256 devices in a mesh: row: 16 (over z, core), cuts: 16 (over x, y).
Axes of the slice: x: 4, y: 4, z: 8, core: 2. Of those that a mesh axis runs over, the one named last changes fastest.
Arguments:
- ham_blocks: bfloat16 [384, 11, 128, 128], P('row'), may hold values from -0.078125 to 0.078125
- neighbors: int32 [384, 11], P('row'), may hold values from 0 to 383, as said below
- slice_widths: int32 [12], replicated, may hold values from 128 to 256, as said below
- interval_index: int32 [12], replicated, may hold values from 0 to 7
- start_vectors: bfloat16 [49152, 2048], P(('row', 'cuts'))
Outputs:
- corrected: bfloat16 [49152, 2048], P(('row', 'cuts'))
The draws below stay inside these ranges and needn't reach their ends.
Inputs may be any that keep to these rules, and one draw needn't show every extreme that they name: `neighbors`: slot 0 of row block b is b, slots 1 and 2 are b + 8 and b - 8 modulo 384, every slot lies within 8 blocks of b modulo 384, and the 11 slots of a row block name distinct block columns. `slice_widths`: every slice holds 128 or 256 vectors, exactly four hold 256, and two of those stand side by side.
All inputs are finite; a program needn't handle non-finite values.
Results may differ from the reference program's by a relative error of at most 0.018.
Values may be sent and summed in bfloat16 or wider, within the bound.
No kernel may reach another device: no remote copies, remote signals or barrier semaphores. Data moves between devices by JAX's collectives and lax.ppermute only.
A program may use at most 64 MiB of HBM per device.

```python
import math
import jax
import jax.numpy as jnp
from jax import lax

BS = 128
NNB = 11
HB = 8
NV = 2048
NSLICE = 12
NINT = 8
NBLK = 384
NROWS = 49152


def draw_neighbors(key, part):
    blocks = jnp.arange(NBLK, dtype=jnp.int32)[:, None]
    fixed_offsets = jnp.broadcast_to(jnp.array([0, HB, -HB], dtype=jnp.int32)[None, :], (NBLK, 3))
    inner = jnp.arange(1, HB, dtype=jnp.int32)
    candidates = jnp.concatenate([inner, -inner]).astype(jnp.int32)
    row_keys = jax.random.split(jax.random.fold_in(key, 11), NBLK)
    shuffled = jax.vmap(lambda row_key: jax.random.permutation(row_key, candidates))(row_keys)
    offsets = jnp.concatenate([fixed_offsets, shuffled[:, :NNB - 3].astype(jnp.int32)], axis=1)
    return jnp.mod(blocks + offsets, NBLK).astype(jnp.int32)


def draw_slice_widths(key, part):
    pair_key, order_key = jax.random.split(jax.random.fold_in(key, 23))
    begin = jax.random.randint(pair_key, (), 0, NSLICE - 1).astype(jnp.int32)
    scores = jax.random.permutation(order_key, NSLICE).astype(jnp.int32) + 2
    places = jnp.arange(NSLICE, dtype=jnp.int32)
    scores = jnp.where((places == begin) | (places == begin + 1), 0, scores)
    order = jnp.argsort(scores, stable=True)
    wide_slots = jnp.zeros((NSLICE,), jnp.int32).at[order[:4]].set(1)
    return (128 + 128 * wide_slots).astype(jnp.int32)


def draw_start_vectors(key, part):
    keys = jax.random.split(jax.random.fold_in(key, 37), 5)
    noise = jax.random.normal(keys[0], (NROWS, NV), jnp.float32)
    common = 0.5
    basis = jax.random.normal(keys[1], (NROWS, 64), jnp.float32)
    mixing = jax.random.normal(keys[2], (64, NV), jnp.float32) * math.sqrt(common / 64.0)
    fraction = jnp.arange(NROWS, dtype=jnp.float32)[:, None] / NROWS
    row_scale = jnp.exp(math.log(3.0) * fraction) * jnp.exp(jax.random.uniform(keys[3], (NROWS, 1), jnp.float32, 0.0, math.log(4.0)))
    col_scale = jnp.exp(jax.random.uniform(keys[4], (1, NV), jnp.float32, 0.0, math.log(10.0)))
    values = (noise + jnp.dot(basis, mixing)) * row_scale * col_scale
    return values.astype(jnp.bfloat16)


def plant(values, own_key, least, high):
    index_at = [jax.random.randint(jax.random.fold_in(own_key, axis), (), 0, length) for axis, length in enumerate(values.shape)]
    widest = values.shape.index(max(values.shape))
    next_to = index_at[:widest] + [(index_at[widest] + 1) % values.shape[widest]] + index_at[widest + 1:]
    return values.at[tuple(index_at)].set(least).at[tuple(next_to)].set(high)


def shard_levels(own_key, dims, pieces, least, high):
    def one(dim, blocks):
        heights = jax.random.uniform(jax.random.fold_in(jax.random.fold_in(own_key, 6), dim), (blocks,), jnp.float32, least / len(pieces), high / len(pieces))
        return jnp.repeat(jnp.exp(heights), dims[dim] // blocks).reshape((-1,) + (1,) * (len(dims) - dim - 1))

    factor_of = one(*pieces[0])
    for cut in pieces[1:]:
        factor_of = factor_of * one(*cut)
    return factor_of


def normal_values(own_key, extent, deviation, limit, shards=(), kind=jnp.bfloat16):
    entries = deviation * jax.random.normal(own_key, extent, jnp.float32)
    if shards:
        entries = entries * shard_levels(own_key, extent, shards, -0.22, 0.18)
    return jnp.clip(entries, -limit, limit).astype(kind)


def setup_inputs(seed: int = 0) -> dict:
    key_list = jax.random.split(jax.random.key(seed), 6)
    return {
        "ham_blocks": normal_values(key_list[0], (NBLK, NNB, BS, BS), (4 * NNB * BS) ** -0.5, 0.078125, ((0, 16),)),
        "neighbors": draw_neighbors(jax.random.fold_in(key_list[5], 71), 0),
        "slice_widths": draw_slice_widths(jax.random.fold_in(key_list[5], 71), 0),
        "interval_index": plant(jax.random.randint(key_list[3], (NSLICE,), 0, NINT), jax.random.fold_in(key_list[3], 1), 0, NINT - 1).astype(jnp.int32),
        "start_vectors": draw_start_vectors(jax.random.fold_in(key_list[5], 71), 0),
    }


def slice_index(columns, bounds):
    return lax.optimization_barrier(jnp.sum((columns[:, None] >= bounds[None, :]).astype(jnp.int32), axis=1)).astype(jnp.int32)

def reference(ham_blocks, neighbors, slice_widths, interval_index, start_vectors):
    bounds = jnp.cumsum(slice_widths).astype(jnp.int32)
    columns = jnp.arange(NV, dtype=jnp.int32)
    slice_of = slice_index(columns, bounds)
    onehot = (slice_of[:, None] == jnp.arange(NSLICE, dtype=jnp.int32)[None, :]).astype(jnp.float32)
    centre = -0.5 + jnp.dot(onehot, interval_index.astype(jnp.float32), precision=lax.Precision.HIGHEST) / (NINT - 1)

    def apply_ham(field):
        stacked = field.reshape(NBLK, BS, NV)

        def one_block(pair):
            blocks, targets = pair
            picked = stacked[targets]
            return jnp.einsum('nij,njw->iw', blocks.astype(jnp.float32), picked.astype(jnp.float32), precision=lax.Precision.HIGHEST)
        return lax.map(one_block, (ham_blocks, neighbors)).reshape(NROWS, NV)
    start = start_vectors
    first = (apply_ham(start) - centre[None, :] * start.astype(jnp.float32)).astype(jnp.bfloat16)
    second = (2.0 * (apply_ham(first) - centre[None, :] * first.astype(jnp.float32)) - start.astype(jnp.float32)).astype(jnp.bfloat16)
    filtered = (2.0 * (apply_ham(second) - centre[None, :] * second.astype(jnp.float32)) - first.astype(jnp.float32)).astype(jnp.bfloat16)
    adjacent = jnp.abs(slice_of[:, None] - slice_of[None, :]) <= 1
    gram = jnp.dot(filtered.T, filtered, preferred_element_type=jnp.float32)
    squares = lax.optimization_barrier(jnp.sum(jnp.square(filtered.astype(jnp.float32)), axis=0))
    inv_norm = lax.rsqrt(squares / NROWS + 1e-05)
    normed = gram * inv_norm[:, None] * inv_norm[None, :] / NROWS
    diagonal_mask = (columns[:, None] == columns[None, :]).astype(jnp.float32)
    coefficients = jnp.where(adjacent, 1.5 * diagonal_mask - 0.5 * normed, 0.0)
    weights = (inv_norm[:, None] * coefficients).astype(jnp.bfloat16)
    return jnp.dot(filtered, weights, preferred_element_type=jnp.float32).astype(jnp.bfloat16)
```

```python
import functools

import jax
import jax.numpy as jnp
from jax import lax
from jax.experimental import pallas as pl
from jax.experimental.pallas import tpu as pltpu
from jax.sharding import PartitionSpec as P

HB = 8
BS = 128
NINT = 8
TILE = 128
PAIRS = 42
HALF = PAIRS // 2
REACH = 3
VMEM = pltpu.VMEM
SMEM = pltpu.SMEM


def vmem_spec():
    return pl.BlockSpec(memory_space=VMEM)


def smem_spec():
    return pl.BlockSpec(memory_space=SMEM)


def apply_kernel(scale, pos_ref, centre_ref, ham_ref, stack_ref, prev_ref, out_ref):
    blocks, slots = ham_ref.shape[:2]
    centre = centre_ref[0]

    def tile_at(b, n):
        start = pl.multiple_of(pos_ref[b, n] * BS, BS)
        return stack_ref[pl.ds(start, BS), :]

    def one_block(b, _):
        total = jnp.zeros((BS, TILE), jnp.float32)
        for n in range(0, slots, 2):
            if n + 1 < slots:
                left = jnp.concatenate([ham_ref[b, n], ham_ref[b, n + 1]], axis=1)
                right = jnp.concatenate([tile_at(b, n), tile_at(b, n + 1)], axis=0)
            else:
                left = ham_ref[b, n]
                right = tile_at(b, n)
            total += jnp.dot(left, right, preferred_element_type=jnp.float32)
        here = pl.ds(pl.multiple_of(b * BS, BS), BS)
        own = stack_ref[pl.ds(pl.multiple_of((b + HB) * BS, BS), BS), :].astype(jnp.float32)
        value = total - centre * own
        if scale != 1:
            value = scale * value - prev_ref[here, :].astype(jnp.float32)
        out_ref[here, :] = value.astype(jnp.bfloat16)
        return 0

    lax.fori_loop(0, blocks, one_block, 0)


def gram_kernel(table_ref, field_ref, keep_ref, send_ref, turned_ref):
    tiles = field_ref.shape[0]
    mine = table_ref[PAIRS + 1] * HALF
    for t in range(tiles):
        turned_ref[t] = field_ref[t].T

    def one_pair(m, _):
        def block(at):
            code = table_ref[at]
            low = code // 4
            return jnp.dot(
                turned_ref[low], field_ref[low + code % 4], preferred_element_type=jnp.float32
            )

        keep_ref[m] = block(mine + m)
        send_ref[m] = block(HALF - mine + m).astype(jnp.bfloat16)
        return 0

    lax.fori_loop(0, HALF, one_pair, 0)


def correct_kernel(rows_all, table_ref, field_ref, mine_ref, other_ref, out_ref, total_ref, row_ref, col_ref):
    tiles = field_ref.shape[0]
    count = table_ref[PAIRS]
    mine = table_ref[PAIRS + 1]
    at_row = lax.broadcasted_iota(jnp.int32, (TILE, TILE), 0)
    at_col = lax.broadcasted_iota(jnp.int32, (TILE, TILE), 1)
    eye = (at_row == at_col).astype(jnp.float32)

    def load(ref, m):
        return ref[m].astype(jnp.float32)

    def each(m, act):
        half = m // HALF
        index = m - half * HALF

        @pl.when(half == mine)
        def _():
            act(load(mine_ref, index))

        @pl.when(half != mine)
        def _():
            act(load(other_ref, index))

    total_ref[...] = jnp.zeros_like(total_ref)

    def norms(m, _):
        code = table_ref[m]
        low = code // 4

        @pl.when(code % 4 == 0)
        def _():
            def act(block):
                diagonal = block * eye
                across = jnp.sum(diagonal, axis=0, keepdims=True)
                down = jnp.sum(diagonal, axis=1, keepdims=True)
                row_ref[low] = jnp.broadcast_to(lax.rsqrt(across / rows_all + 1e-05), (8, TILE))
                col_ref[low] = jnp.broadcast_to(lax.rsqrt(down / rows_all + 1e-05), (TILE, TILE))

            each(m, act)

        return 0

    lax.fori_loop(0, count, norms, 0)

    def one_pair(m, _):
        code = table_ref[m]
        low = code // 4
        step = code % 4
        high = low + step

        def act(block):
            down = col_ref[low]
            across = row_ref[high][:1]
            normed = block * down * across / rows_all
            same = (step == 0).astype(jnp.float32)
            coefficient = 1.5 * (eye * same) - 0.5 * normed
            forward = (down * coefficient).astype(jnp.bfloat16)
            total_ref[high] += jnp.dot(field_ref[low], forward, preferred_element_type=jnp.float32)

            @pl.when(step != 0)
            def _():
                backward = (across * coefficient).astype(jnp.bfloat16)
                total_ref[low] += lax.dot_general(
                    field_ref[high],
                    backward,
                    (((1,), (1,)), ((), ())),
                    preferred_element_type=jnp.float32,
                )

        each(m, act)
        return 0

    lax.fori_loop(0, count, one_pair, 0)
    for t in range(tiles):
        out_ref[:, t * TILE : (t + 1) * TILE] = total_ref[t].astype(jnp.bfloat16)


def shift(array, distance):
    size = lax.axis_size("row")
    return lax.ppermute(array, "row", [(i, (i + distance) % size) for i in range(size)])


def exchange(array, bit):
    return lax.ppermute(array, "row", [(i, i ^ bit) for i in range(lax.axis_size("row"))])


def body(ham_blocks, neighbors, slice_widths, interval_index, start_vectors):
    rows_mine, columns = start_vectors.shape
    tiles = columns // TILE
    blocks, slots = ham_blocks.shape[:2]
    row_count = lax.axis_size("row")
    rows_all = blocks * BS * row_count
    panel = lax.all_to_all(start_vectors, "cuts", split_axis=1, concat_axis=0, tiled=True)

    first_block = lax.axis_index("row") * blocks
    position = jnp.mod(neighbors - first_block + HB, blocks * row_count)
    core = lax.axis_index("row") % 2
    ends = jnp.cumsum(slice_widths) // TILE
    tile = jnp.arange(tiles, dtype=jnp.int32)
    slice_of = jnp.sum((tile[:, None] >= ends[None, :]).astype(jnp.int32), axis=1)
    own_slice = jnp.sum(jnp.where(tile == lax.axis_index("cuts"), slice_of, 0))
    at_slice = jnp.arange(slice_widths.shape[0], dtype=jnp.int32)
    interval = jnp.sum(jnp.where(at_slice == own_slice, interval_index, 0))
    centre = (-0.5 + interval.astype(jnp.float32) / (NINT - 1)).reshape(1)

    code = jnp.arange(tiles * 4, dtype=jnp.int32)
    low, step = code // 4, code % 4
    def slice_at(index):
        return jnp.sum((index[:, None] * TILE >= (ends * TILE)[None, :]).astype(jnp.int32), axis=1)
    valid = (low + step < tiles) & (slice_at(low + step) - slice_at(low) <= 1)
    rank = jnp.sum((valid[None, :] & (code[None, :] < code[:, None])).astype(jnp.int32), axis=1)
    places = jnp.arange(PAIRS, dtype=jnp.int32)
    listed = jnp.sum(
        jnp.where(valid[None, :] & (rank[None, :] == places[:, None]), code[None, :], 0), axis=1
    )
    table = jnp.concatenate(
        [listed, jnp.sum(valid.astype(jnp.int32)).reshape(1), core.reshape(1)]
    ).astype(jnp.int32)

    def apply_ham(scale, field, before):
        width = HB * BS
        low_side = shift(field[-width:], 1)
        high_side = shift(field[:width], -1)
        stack = jnp.concatenate([low_side, field, high_side], axis=0)
        return pl.pallas_call(
            functools.partial(apply_kernel, scale),
            out_shape=jax.ShapeDtypeStruct(field.shape, jnp.bfloat16),
            in_specs=[smem_spec(), smem_spec(), vmem_spec(), vmem_spec(), vmem_spec()],
            out_specs=vmem_spec(),
        )(position, centre, ham_blocks, stack, before)

    first = apply_ham(1, panel, panel)
    second = apply_ham(2, first, panel)
    filtered = apply_ham(2, second, first)

    field = lax.all_to_all(filtered.reshape(tiles, rows_mine, TILE), "cuts", 0, 0)
    kept, sent = pl.pallas_call(
        gram_kernel,
        out_shape=(
            jax.ShapeDtypeStruct((HALF, TILE, TILE), jnp.float32),
            jax.ShapeDtypeStruct((HALF, TILE, TILE), jnp.bfloat16),
        ),
        in_specs=[smem_spec(), vmem_spec()],
        out_specs=(vmem_spec(), vmem_spec()),
        scratch_shapes=[VMEM((tiles, TILE, rows_mine), jnp.bfloat16)],
    )(table, field)
    partial = (kept + exchange(sent, 1).astype(jnp.float32)).astype(jnp.bfloat16)
    cut_count = lax.axis_size("cuts")
    share = HALF * TILE // cut_count
    pieces = lax.all_to_all(partial.reshape(cut_count, share, TILE), "cuts", 0, 0)
    total = jnp.sum(pieces.astype(jnp.float32), axis=0)
    bit = 2
    while bit < row_count:
        rounded = total.astype(jnp.bfloat16)
        total = rounded.astype(jnp.float32) + exchange(rounded, bit).astype(jnp.float32)
        bit *= 2
    spread = jnp.broadcast_to(total.astype(jnp.bfloat16)[None], (cut_count, share, TILE))
    mine = lax.all_to_all(spread, "cuts", 0, 0).reshape(HALF, TILE, TILE)
    other = exchange(mine, 1)
    return pl.pallas_call(
        functools.partial(correct_kernel, rows_all),
        out_shape=jax.ShapeDtypeStruct((rows_mine, columns), jnp.bfloat16),
        in_specs=[smem_spec(), vmem_spec(), vmem_spec(), vmem_spec()],
        out_specs=vmem_spec(),
        scratch_shapes=[
            VMEM((tiles, rows_mine, TILE), jnp.float32),
            VMEM((tiles, 8, TILE), jnp.float32),
            VMEM((tiles, TILE, TILE), jnp.float32),
        ],
    )(table, field, mine, other)


def solution(mesh):
    return jax.shard_map(
        body,
        mesh=mesh,
        in_specs=(P("row", None, None, None), P("row", None), P(), P(), P(("row", "cuts"), None)),
        out_specs=P(("row", "cuts"), None),
        check_vma=False,
    )
```

```python
import functools

import jax
import jax.numpy as jnp
from jax import lax
from jax.experimental import pallas as pl
from jax.experimental.pallas import tpu as pltpu
from jax.sharding import PartitionSpec as P

HB = 8
BS = 128
NINT = 8
TILE = 128
PAIRS = 42
HALF = PAIRS // 2
REACH = 4
VMEM = pltpu.VMEM
SMEM = pltpu.SMEM
F32 = jnp.float32
BF16 = jnp.bfloat16


def vmem(count):
    return [pl.BlockSpec(memory_space=VMEM)] * count


def smem(count):
    return [pl.BlockSpec(memory_space=SMEM)] * count


def call(kernel, outs, scalars, arrays, scratch=(), flops=0, limit=24 << 20):
    moved = sum(a.size * a.dtype.itemsize for a in (*arrays, *outs))
    return pl.pallas_call(
        kernel,
        out_shape=tuple(outs),
        in_specs=smem(len(scalars)) + vmem(len(arrays)),
        out_specs=tuple(vmem(len(outs))),
        scratch_shapes=list(scratch),
        compiler_params=pltpu.CompilerParams(vmem_limit_bytes=limit),
        cost_estimate=pl.CostEstimate(flops=flops, bytes_accessed=moved, transcendentals=0),
    )(*scalars, *arrays)


def shape(dims, dtype=BF16):
    return jax.ShapeDtypeStruct(dims, dtype)


def table_kernel(where_ref, turned_ref, width_ref, interval_ref, near_ref, far_ref, pair_ref):
    slots, blocks = turned_ref.shape
    first, total, cut = where_ref[0], where_ref[1], where_ref[2]
    edge = blocks // 3

    def one_row(b, _):
        line = jnp.where(b < edge, b, b - edge)
        outer = (b < edge) | (b >= 2 * edge)

        @pl.when(outer)
        def _():
            for k in range(edge):
                far_ref[line, k] = edge

        found = jnp.int32(0)
        for n in range(slots):
            away = turned_ref[n, b] - first
            away = jnp.where(away < -HB, away + total, away)
            away = jnp.where(away >= total - HB, away - total, away)
            local = (away >= 0) & (away < blocks)
            near_ref[n, b] = jnp.where(local, away, blocks)
            halo = jnp.where(away < 0, away + HB, away - blocks)

            @pl.when(jnp.logical_not(local))
            def _():
                far_ref[line, found] = n * 16 + halo

            found += jnp.where(local, 0, 1)
        return 0

    lax.fori_loop(0, blocks, one_row, 0)
    tiles = (pair_ref.shape[0] - 2) // REACH
    ends = []
    end = jnp.int32(0)
    for s in range(width_ref.shape[0]):
        end += width_ref[s] // TILE
        ends.append(end)

    def slice_of(t):
        index = jnp.int32(0)
        for end in ends:
            index += jnp.where(t >= end, 1, 0)
        return index

    lanes = [slice_of(t) for t in range(tiles)]
    slot = jnp.int32(0)
    for i in range(tiles):
        for d in range(REACH):
            if i + d < tiles:
                valid = lanes[i + d] - lanes[i] <= 1
                pair_ref[i * REACH + d] = jnp.where(valid, slot, PAIRS)
                slot += jnp.where(valid, 1, 0)
            else:
                pair_ref[i * REACH + d] = PAIRS
    pair_ref[tiles * REACH] = where_ref[3]
    pair_ref[tiles * REACH + 1] = interval_ref[slice_of(cut)]


def near_kernel(scale, near_ref, pair_ref, ham_ref, low_ref, mid_ref, high_ref, *rest):
    before = rest[:3] if scale != 1 else None
    mid_out, low_out, high_out, stack = rest[-4:]
    blocks, slots = ham_ref.shape[:2]
    third = blocks // 3
    span = third * BS
    for q, ref in enumerate((low_ref, mid_ref, high_ref)):
        stack[q * span : (q + 1) * span] = ref[...]
    stack[blocks * BS :] = jnp.zeros((BS, TILE), BF16)
    centre = -0.5 + pair_ref[pair_ref.shape[0] - 1].astype(F32) * F32(1 / (NINT - 1))

    def tile_at(n, b):
        return stack[pl.ds(pl.multiple_of(near_ref[n, b] * BS, BS), BS), :]

    for b in (*range(third), *range(2 * third, blocks), *range(third, 2 * third)):
        total = jnp.zeros((BS, TILE), F32)
        for n in range(0, slots, 2):
            if n + 1 < slots:
                left = jnp.concatenate([ham_ref[b, n], ham_ref[b, n + 1]], axis=1)
                right = jnp.concatenate([tile_at(n, b), tile_at(n + 1, b)], axis=0)
            else:
                left, right = ham_ref[b, n], tile_at(n, b)
            total += jnp.dot(left, right, preferred_element_type=F32)
        part = b // third
        here = slice((b - part * third) * BS, (b - part * third + 1) * BS)
        own = stack[b * BS : (b + 1) * BS].astype(F32)
        value = total - centre * own
        if scale != 1:
            value = scale * value - before[part][here, :].astype(F32)
        out = (low_out, mid_out, high_out)[part]
        out[here, :] = value.astype(out.dtype)


def far_kernel(scale, joined, far_ref, ham_ref, below_ref, above_ref, low_ref, high_ref, *rest):
    stack = rest[-1]
    span = below_ref.shape[0]
    edge = span // BS
    for q, ref in enumerate((below_ref, above_ref)):
        stack[q, :span] = ref[...]
        stack[q, span:] = jnp.zeros((BS, TILE), BF16)
    for line in range(2 * edge):
        side = line // edge
        index = line - side * edge
        b = index + side * 2 * edge
        most = edge - index if side == 0 else index + 1
        left, right = [], []
        for k in range(most):
            entry = far_ref[line, k]
            slot = entry // 16
            left.append(ham_ref[b, slot])
            start = pl.multiple_of((entry - slot * 16) * BS, BS)
            right.append(stack[side, pl.ds(start, BS), :])
        total = (low_ref, high_ref)[side][index * BS : (index + 1) * BS, :]
        for k in range(0, most, 2):
            lhs = jnp.concatenate(left[k : k + 2], axis=1)
            rhs = jnp.concatenate(right[k : k + 2], axis=0)
            total += scale * jnp.dot(lhs, rhs, preferred_element_type=F32)
        value = total.astype(BF16)
        if joined:
            rest[-2][b * BS : (b + 1) * BS, :] = value
        else:
            rest[side][index * BS : (index + 1) * BS, :] = value
    if joined:
        rest[-2][span : 2 * span, :] = rest[0][...]


def gram_kernel(pair_ref, field_ref, keep_ref, send_ref):
    tiles = field_ref.shape[0]
    core = pair_ref[tiles * REACH]
    mine = core * HALF
    theirs = HALF - mine
    for i in range(tiles):
        reach = min(REACH, tiles - i)
        right = jnp.concatenate([field_ref[i + d] for d in range(reach)], axis=1)
        block = lax.dot_general(
            field_ref[i], right, (((0,), (0,)), ((), ())), preferred_element_type=F32
        )
        for d in range(reach):
            slot = pair_ref[i * REACH + d]
            piece = block[:, d * TILE : (d + 1) * TILE]

            @pl.when((slot >= mine) & (slot < mine + HALF))
            def _():
                keep_ref[slot - mine] = piece

            @pl.when((slot >= theirs) & (slot < theirs + HALF))
            def _():
                send_ref[slot - theirs] = piece.astype(BF16)


def correct_kernel(rows_all, pair_ref, field_ref, mine_ref, other_ref, out_ref, gram, scaled, norm):
    tiles = field_ref.shape[0]
    core = pair_ref[tiles * REACH]
    gram[pl.ds(core * HALF, HALF)] = mine_ref[...]
    gram[pl.ds(HALF - core * HALF, HALF)] = other_ref[...]
    gram[PAIRS] = jnp.zeros((TILE, TILE), BF16)
    at_row = lax.broadcasted_iota(jnp.int32, (TILE, TILE), 0)
    at_col = lax.broadcasted_iota(jnp.int32, (TILE, TILE), 1)
    eye = at_row == at_col
    for t in range(tiles):
        block = gram[pair_ref[t * REACH]].astype(F32)
        squares = jnp.sum(jnp.where(eye, block, 0.0), axis=0, keepdims=True)
        inverse = lax.rsqrt(squares / rows_all + 1e-05)
        norm[t : t + 1, :] = inverse
        scaled[t] = (field_ref[t].astype(F32) * (inverse * inverse)).astype(BF16)
    for j in range(tiles):
        below = range(max(0, j - REACH + 1), j + 1)
        left = jnp.concatenate([scaled[i] for i in below], axis=1)
        right = jnp.concatenate([gram[pair_ref[i * REACH + j - i]] for i in below], axis=0)
        total = jnp.dot(left, right, preferred_element_type=F32)
        above = range(j + 1, min(tiles, j + REACH))
        if above:
            left = jnp.concatenate([scaled[i] for i in above], axis=1)
            right = jnp.concatenate([gram[pair_ref[j * REACH + i - j]] for i in above], axis=1)
            total += lax.dot_general(
                left, right, (((1,), (1,)), ((), ())), preferred_element_type=F32
            )
        value = norm[j : j + 1, :] * (1.5 * field_ref[j].astype(F32) - (0.5 / rows_all) * total)
        out_ref[:, j * TILE : (j + 1) * TILE] = value.astype(BF16)


def shift(array, distance):
    size = lax.axis_size("row")
    return lax.ppermute(array, "row", [(i, (i + distance) % size) for i in range(size)])


def exchange(array, bit):
    return lax.ppermute(array, "row", [(i, i ^ bit) for i in range(lax.axis_size("row"))])


def body(ham_blocks, neighbors, slice_widths, interval_index, start_vectors):
    rows_mine, columns = start_vectors.shape
    tiles = columns // TILE
    blocks, slots = ham_blocks.shape[:2]
    row_count = lax.axis_size("row")
    rows_all = blocks * BS * row_count
    panel_rows = blocks * BS
    span = panel_rows // 3
    panel = lax.all_to_all(start_vectors, "cuts", split_axis=1, concat_axis=0, tiled=True)

    row = lax.axis_index("row")
    place = jnp.stack(
        [row * blocks, jnp.int32(blocks * row_count), lax.axis_index("cuts"), row % 2]
    ).astype(jnp.int32)
    near, far, pair = pl.pallas_call(
        table_kernel,
        out_shape=(
            shape((slots, blocks), jnp.int32),
            shape((2 * blocks // 3, HB), jnp.int32),
            shape((tiles * REACH + 2,), jnp.int32),
        ),
        in_specs=smem(4),
        out_specs=tuple(smem(3)),
        cost_estimate=pl.CostEstimate(flops=1 << 20, bytes_accessed=1 << 12, transcendentals=0),
    )(place, neighbors.T, slice_widths, interval_index)
    ham = pltpu.with_memory_space_constraint(ham_blocks, VMEM)
    work = 2 * blocks * slots * BS * BS * TILE

    def apply_ham(scale, field, before, joined):
        low, mid, high = field
        below = shift(high, 1)
        above = shift(low, -1)
        mid, low, high = call(
            functools.partial(near_kernel, scale),
            [shape((span, TILE)), shape((span, TILE), F32), shape((span, TILE), F32)],
            [near, pair],
            [ham, low, mid, high, *before],
            [VMEM((panel_rows + BS, TILE), BF16)],
            work,
        )
        outs = [shape((panel_rows, TILE))] if joined else [shape((span, TILE))] * 2
        result = call(
            functools.partial(far_kernel, scale, joined),
            outs,
            [far],
            [ham, below, above, low, high] + [mid] * joined,
            [VMEM((2, span + BS, TILE), BF16)],
            work // 4,
        )
        return result[0] if joined else (result[0], mid, result[1])

    start = tuple(panel[q * span : (q + 1) * span] for q in range(3))
    first = apply_ham(1, start, (), False)
    second = apply_ham(2, first, start, False)
    filtered = apply_ham(2, second, first, True)

    field = lax.all_to_all(filtered.reshape(tiles, rows_mine, TILE), "cuts", 0, 0)
    kept, sent = call(
        gram_kernel,
        [shape((HALF, TILE, TILE), F32), shape((HALF, TILE, TILE))],
        [pair],
        [field],
        (),
        1 << 28,
    )
    partial = (kept + exchange(sent, 1).astype(F32)).astype(BF16)
    cut_count = lax.axis_size("cuts")
    share = HALF * TILE // cut_count
    pieces = lax.all_to_all(partial.reshape(cut_count, share, TILE), "cuts", 0, 0)
    total = jnp.sum(pieces.astype(F32), axis=0)
    bit = 2
    while bit < row_count:
        rounded = total.astype(BF16)
        total = rounded.astype(F32) + exchange(rounded, bit).astype(F32)
        bit *= 2
    spread = jnp.broadcast_to(total.astype(BF16)[None], (cut_count, share, TILE))
    mine = lax.all_to_all(spread, "cuts", 0, 0).reshape(HALF, TILE, TILE)
    other = exchange(mine, 1)
    (corrected,) = call(
        functools.partial(correct_kernel, rows_all),
        [shape((rows_mine, columns))],
        [pair],
        [field, mine, other],
        [
            VMEM((PAIRS + 1, TILE, TILE), BF16),
            VMEM((tiles, rows_mine, TILE), BF16),
            VMEM((tiles, TILE), F32),
        ],
        1 << 29,
    )
    return corrected


def solution(mesh):
    return jax.shard_map(
        body,
        mesh=mesh,
        in_specs=(P("row", None, None, None), P("row", None), P(), P(), P(("row", "cuts"), None)),
        out_specs=P(("row", "cuts"), None),
        check_vma=False,
    )
```

```python
import functools

import jax
import jax.numpy as jnp
from jax import lax
from jax.experimental import pallas as pl
from jax.experimental.pallas import tpu as pltpu
from jax.sharding import PartitionSpec as P

HB = 8
BS = 128
NINT = 8
TILE = 128
PAIRS = 42
HALF = PAIRS // 2
REACH = 4
VMEM = pltpu.VMEM
SMEM = pltpu.SMEM
F32 = jnp.float32
BF16 = jnp.bfloat16


def vmem(count):
    return [pl.BlockSpec(memory_space=VMEM)] * count


def smem(count):
    return [pl.BlockSpec(memory_space=SMEM)] * count


def call(kernel, outs, scalars, arrays, scratch=(), flops=0, limit=24 << 20):
    moved = sum(a.size * a.dtype.itemsize for a in (*arrays, *outs))
    return pl.pallas_call(
        kernel,
        out_shape=tuple(outs),
        in_specs=smem(len(scalars)) + vmem(len(arrays)),
        out_specs=tuple(vmem(len(outs))),
        scratch_shapes=list(scratch),
        compiler_params=pltpu.CompilerParams(vmem_limit_bytes=limit),
        cost_estimate=pl.CostEstimate(flops=flops, bytes_accessed=moved, transcendentals=0),
    )(*scalars, *arrays)


def shape(dims, dtype=BF16):
    return jax.ShapeDtypeStruct(dims, dtype)


def table_kernel(where_ref, turned_ref, width_ref, interval_ref, near_ref, far_ref, pair_ref, list_ref):
    slots, blocks = turned_ref.shape
    first, total, cut = where_ref[0], where_ref[1], where_ref[2]
    edge = blocks // 3

    def one_row(b, _):
        line = jnp.where(b < edge, b, b - edge)
        outer = (b < edge) | (b >= 2 * edge)

        @pl.when(outer)
        def _():
            for k in range(edge):
                far_ref[line, k] = edge

        found = jnp.int32(0)
        for n in range(slots):
            away = turned_ref[n, b] - first
            away = jnp.where(away < -HB, away + total, away)
            away = jnp.where(away >= total - HB, away - total, away)
            local = (away >= 0) & (away < blocks)
            near_ref[n, b] = jnp.where(local, away, blocks)
            halo = jnp.where(away < 0, away + HB, away - blocks)

            @pl.when(jnp.logical_not(local))
            def _():
                far_ref[line, found] = n * 16 + halo

            found += jnp.where(local, 0, 1)
        return 0

    lax.fori_loop(0, blocks, one_row, 0)
    tiles = (pair_ref.shape[0] - 2) // REACH
    ends = []
    end = jnp.int32(0)
    for s in range(width_ref.shape[0]):
        end += width_ref[s] // TILE
        ends.append(end)

    def slice_of(t):
        index = jnp.int32(0)
        for end in ends:
            index += jnp.where(t >= end, 1, 0)
        return index

    lanes = [slice_of(t) for t in range(tiles)]
    slot = jnp.int32(0)
    for m in range(PAIRS + 1):
        list_ref[m] = 0
    for i in range(tiles):
        for d in range(REACH):
            if i + d < tiles:
                valid = lanes[i + d] - lanes[i] <= 1
                pair_ref[i * REACH + d] = jnp.where(valid, slot, PAIRS)
                list_ref[jnp.where(valid, slot, PAIRS)] = i * REACH + d
                slot += jnp.where(valid, 1, 0)
            else:
                pair_ref[i * REACH + d] = PAIRS
    pair_ref[tiles * REACH] = where_ref[3]
    pair_ref[tiles * REACH + 1] = interval_ref[slice_of(cut)]


def turn_kernel(start_ref, out_ref, tiles_ref, read, written):
    tiles = out_ref.shape[0]

    def load(t):
        return pltpu.make_async_copy(
            start_ref.at[:, t * TILE : (t + 1) * TILE], tiles_ref.at[t], read.at[t]
        )

    def store(t):
        return pltpu.make_async_copy(tiles_ref.at[t], out_ref.at[t], written.at[t])

    for t in range(tiles):
        load(t).start()
    for t in range(tiles):
        load(t).wait()
        store(t).start()
    for t in range(tiles):
        store(t).wait()


def near_kernel(scale, near_ref, pair_ref, ham_ref, inner_ref, mid_ref, outer_ref, *rest):
    first = scale == 1
    blocks, slots = ham_ref.shape[:2]
    if first:
        mid_out, edge_out, ham_out, stack, loaded = rest
        chunk = blocks // loaded.shape[0]

        def load(c):
            rows = slice(c * chunk, (c + 1) * chunk)
            return pltpu.make_async_copy(ham_ref.at[rows], ham_out.at[rows], loaded.at[c])

        for c in range(blocks // chunk):
            load(c).start()
        ham = ham_out
    else:
        mid_out, edge_out, before, stack = rest[-4:]
        ham = ham_ref
    third = blocks // 3
    span = third * BS
    core = pair_ref[pair_ref.shape[0] - 2]
    inner_at, outer_at = (1 - core) * 2 * span, core * 2 * span

    def spread(inner, mid, outer, into):
        into[pl.ds(pl.multiple_of(inner_at, span), span)] = inner[...]
        into[pl.ds(pl.multiple_of(outer_at, span), span)] = outer[...]
        into[span : 2 * span] = mid[...]

    spread(inner_ref, mid_ref, outer_ref, stack)
    stack[blocks * BS :] = jnp.zeros((BS, TILE), BF16)
    if not first:
        spread(*rest[:3], before)
    centre = -0.5 + pair_ref[pair_ref.shape[0] - 1].astype(F32) * F32(1 / (NINT - 1))

    def tile_at(n, b):
        return stack[pl.ds(pl.multiple_of(near_ref[n, b] * BS, BS), BS), :]

    for b in range(blocks):
        if first and b % chunk == 0:
            load(b // chunk).wait()
        total = jnp.zeros((BS, TILE), F32)
        for n in range(0, slots, 2):
            if n + 1 < slots:
                left = jnp.concatenate([ham[b, n], ham[b, n + 1]], axis=1)
                right = jnp.concatenate([tile_at(n, b), tile_at(n + 1, b)], axis=0)
            else:
                left, right = ham[b, n], tile_at(n, b)
            total += jnp.dot(left, right, preferred_element_type=F32)
        part = b // third
        here = slice((b - part * third) * BS, (b - part * third + 1) * BS)
        own = stack[b * BS : (b + 1) * BS].astype(F32)
        value = total - centre * own
        if not first:
            value = scale * value - before[b * BS : (b + 1) * BS].astype(F32)
        if part == 1:
            mid_out[here, :] = value.astype(BF16)
        else:
            edge_out[part // 2, here, :] = value


def add_halo(scale, far_ref, ham_ref, stack, edge_ref, side, k, edge):
    index = k + side * (edge - 1 - 2 * k)
    b = k + side * (3 * edge - 1 - 2 * k)
    left, right = [], []
    for slot_at in range(edge - k):
        entry = far_ref[side * edge + index, slot_at]
        slot = entry // 16
        left.append(ham_ref[b, slot])
        start = pl.multiple_of((entry - slot * 16) * BS, BS)
        right.append(stack[pl.ds(start, BS), :])
    here = pl.ds(pl.multiple_of(index * BS, BS), BS)
    total = edge_ref[side, here, :]
    for slot_at in range(0, edge - k, 2):
        lhs = jnp.concatenate(left[slot_at : slot_at + 2], axis=1)
        rhs = jnp.concatenate(right[slot_at : slot_at + 2], axis=0)
        total += scale * jnp.dot(lhs, rhs, preferred_element_type=F32)
    return index, total.astype(BF16)


def edge_kernel(scale, outer, far_ref, pair_ref, ham_ref, halo_ref, edge_ref, out_ref, stack):
    span = halo_ref.shape[0]
    edge = span // BS
    core = pair_ref[pair_ref.shape[0] - 2]
    side = core if outer else 1 - core
    stack[:span] = halo_ref[...]
    stack[span:] = jnp.zeros((BS, TILE), BF16)
    for k in range(edge):
        index, value = add_halo(scale, far_ref, ham_ref, stack, edge_ref, side, k, edge)
        out_ref[pl.ds(pl.multiple_of(index * BS, BS), BS), :] = value


def joined_kernel(scale, far_ref, pair_ref, ham_ref, inner_ref, outer_ref, edge_ref, mid_ref, out_ref, stack):
    span = inner_ref.shape[0]
    edge = span // BS
    core = pair_ref[pair_ref.shape[0] - 2]
    for side, ref in ((1 - core, inner_ref), (core, outer_ref)):
        stack[side, :span] = ref[...]
        stack[side, span:] = jnp.zeros((BS, TILE), BF16)
    out_ref[span : 2 * span, :] = mid_ref[...]
    for side in range(2):
        for k in range(edge):
            index, value = add_halo(
                scale, far_ref, ham_ref, stack.at[side], edge_ref, side, k, edge
            )
            at = side * 2 * span + index * BS
            out_ref[at : at + BS, :] = value


def gram_kernel(keep, pair_ref, list_ref, field_ref, out_ref, turned):
    tiles = field_ref.shape[0]
    core = pair_ref[tiles * REACH]
    first = (core if keep else 1 - core) * HALF
    for t in range(tiles):
        turned[t] = field_ref[t].T
    for m in range(HALF):
        code = list_ref[first + m]
        low = code // REACH
        high = low + code - low * REACH
        block = jnp.dot(turned[low], field_ref[high], preferred_element_type=F32)
        out_ref[m] = block.astype(out_ref.dtype)


def correct_kernel(rows_all, pair_ref, field_ref, mine_ref, other_ref, out_ref, gram, scaled, norm):
    tiles = field_ref.shape[0]
    core = pair_ref[tiles * REACH]
    gram[pl.ds(core * HALF, HALF)] = mine_ref[...]
    gram[pl.ds(HALF - core * HALF, HALF)] = other_ref[...]
    gram[PAIRS] = jnp.zeros((TILE, TILE), BF16)
    at_row = lax.broadcasted_iota(jnp.int32, (TILE, TILE), 0)
    at_col = lax.broadcasted_iota(jnp.int32, (TILE, TILE), 1)
    eye = at_row == at_col
    for t in range(tiles):
        block = gram[pair_ref[t * REACH]].astype(F32)
        squares = jnp.sum(jnp.where(eye, block, 0.0), axis=0, keepdims=True)
        inverse = lax.rsqrt(squares / rows_all + 1e-05)
        norm[t : t + 1, :] = inverse
        scaled[t] = (field_ref[t].astype(F32) * (inverse * inverse)).astype(BF16)
    for j in range(tiles):
        below = range(max(0, j - REACH + 1), j + 1)
        left = jnp.concatenate([scaled[i] for i in below], axis=1)
        right = jnp.concatenate([gram[pair_ref[i * REACH + j - i]] for i in below], axis=0)
        total = jnp.dot(left, right, preferred_element_type=F32)
        above = range(j + 1, min(tiles, j + REACH))
        if above:
            left = jnp.concatenate([scaled[i] for i in above], axis=1)
            right = jnp.concatenate([gram[pair_ref[j * REACH + i - j]] for i in above], axis=1)
            total += lax.dot_general(
                left, right, (((1,), (1,)), ((), ())), preferred_element_type=F32
            )
        value = norm[j : j + 1, :] * (1.5 * field_ref[j].astype(F32) - (0.5 / rows_all) * total)
        out_ref[:, j * TILE : (j + 1) * TILE] = value.astype(BF16)


def shift(array, distance):
    size = lax.axis_size("row")
    return lax.ppermute(array, "row", [(i, (i + distance) % size) for i in range(size)])


def exchange(array):
    return lax.ppermute(array, "row", [(i, i ^ 1) for i in range(lax.axis_size("row"))])


def swap_outer(array):
    size = lax.axis_size("row")
    return lax.ppermute(array, "row", [(i, (i - 1 + 2 * (i % 2)) % size) for i in range(size)])


def ring_total(piece):
    own = piece.astype(F32)
    pair = own + shift(piece, -2).astype(F32)
    three = pair + shift(piece, 2).astype(F32)
    after = shift(three.astype(BF16), -6).astype(F32)
    before = shift(pair.astype(BF16), 6).astype(F32)
    return three + after + before


def body(ham_blocks, neighbors, slice_widths, interval_index, start_vectors):
    rows_mine, columns = start_vectors.shape
    tiles = columns // TILE
    blocks, slots = ham_blocks.shape[:2]
    row_count = lax.axis_size("row")
    rows_all = blocks * BS * row_count
    panel_rows = blocks * BS
    span = panel_rows // 3
    turned = pl.pallas_call(
        turn_kernel,
        out_shape=shape((tiles, rows_mine, TILE)),
        in_specs=[pl.BlockSpec(memory_space=pltpu.HBM)],
        out_specs=pl.BlockSpec(memory_space=pltpu.HBM),
        scratch_shapes=[
            VMEM((tiles, rows_mine, TILE), BF16),
            pltpu.SemaphoreType.DMA((tiles,)),
            pltpu.SemaphoreType.DMA((tiles,)),
        ],
        compiler_params=pltpu.CompilerParams(vmem_limit_bytes=62 << 20),
    )(start_vectors)
    panel = lax.all_to_all(turned, "cuts", 0, 0).reshape(panel_rows, TILE)

    row = lax.axis_index("row")
    place = jnp.stack(
        [row * blocks, jnp.int32(blocks * row_count), lax.axis_index("cuts"), row % 2]
    ).astype(jnp.int32)
    near, far, pair, listed = pl.pallas_call(
        table_kernel,
        out_shape=(
            shape((slots, blocks), jnp.int32),
            shape((2 * blocks // 3, HB), jnp.int32),
            shape((tiles * REACH + 2,), jnp.int32),
            shape((PAIRS + 1,), jnp.int32),
        ),
        in_specs=smem(4),
        out_specs=tuple(smem(4)),
        compiler_params=pltpu.CompilerParams(vmem_limit_bytes=1 << 20),
        cost_estimate=pl.CostEstimate(flops=1 << 20, bytes_accessed=1 << 12, transcendentals=0),
    )(place, neighbors.T, slice_widths, interval_index)
    panel, near, far, pair, listed = lax.optimization_barrier((panel, near, far, pair, listed))
    work = 2 * blocks * slots * BS * BS * TILE
    outs = [shape((span, TILE)), shape((2, span, TILE), F32)]
    stacks = [VMEM((panel_rows, TILE), BF16), VMEM((panel_rows + BS, TILE), BF16)]

    def halos(inner, outer):
        from_outer = swap_outer(outer)
        return exchange(inner), from_outer

    def apply_first(field):
        inner, mid, outer = field
        from_inner, from_outer = halos(inner, outer)
        mid, edges, ham = pl.pallas_call(
            functools.partial(near_kernel, 1),
            out_shape=(*outs, shape(ham_blocks.shape)),
            in_specs=smem(2) + [pl.BlockSpec(memory_space=pltpu.HBM)] + vmem(3),
            out_specs=tuple(vmem(3)),
            scratch_shapes=[stacks[1], pltpu.SemaphoreType.DMA((blocks // 3,))],
            compiler_params=pltpu.CompilerParams(vmem_limit_bytes=40 << 20),
            cost_estimate=pl.CostEstimate(
                flops=work, bytes_accessed=ham_blocks.size * 2, transcendentals=0
            ),
        )(near, pair, ham_blocks, inner, mid, outer)
        ham = pltpu.with_memory_space_constraint(ham, VMEM)
        return ham, (from_inner, from_outer, edges, mid)

    def apply_next(ham, field, before):
        inner, mid, outer = field
        from_inner, from_outer = halos(inner, outer)
        mid, edges = call(
            functools.partial(near_kernel, 2),
            outs,
            [near, pair],
            [ham, inner, mid, outer, *before],
            stacks,
            work,
        )
        return from_inner, from_outer, edges, mid

    def edges_of(scale, ham, from_inner, from_outer, edges, mid):
        def side(outer, halo):
            (out,) = call(
                functools.partial(edge_kernel, scale, outer),
                [shape((span, TILE))],
                [far, pair],
                [ham, halo, edges],
                [VMEM((span + BS, TILE), BF16)],
                work // 8,
            )
            return out

        outer = side(True, from_outer)
        return side(False, from_inner), mid, outer

    low, mid, high = (panel[q * span : (q + 1) * span] for q in range(3))
    even = row % 2 == 0
    start = (jnp.where(even, high, low), mid, jnp.where(even, low, high))
    ham, parts = apply_first(start)
    first = edges_of(1, ham, *parts)
    second = edges_of(2, ham, *apply_next(ham, first, start))
    from_inner, from_outer, edges, mid = apply_next(ham, second, first)
    (filtered,) = call(
        functools.partial(joined_kernel, 2),
        [shape((panel_rows, TILE))],
        [far, pair],
        [ham, from_inner, from_outer, edges, mid],
        [VMEM((2, span + BS, TILE), BF16)],
        work // 4,
    )

    field = lax.all_to_all(filtered.reshape(tiles, rows_mine, TILE), "cuts", 0, 0)

    def gram(keep):
        (out,) = call(
            functools.partial(gram_kernel, keep),
            [shape((HALF, TILE, TILE), F32 if keep else BF16)],
            [pair, listed],
            [field],
            [VMEM((tiles, TILE, rows_mine), BF16)],
            1 << 28,
        )
        return out

    partial = (gram(True) + exchange(gram(False)).astype(F32)).astype(BF16)
    cut_count = lax.axis_size("cuts")
    share = HALF * TILE // cut_count
    pieces = lax.all_to_all(partial.reshape(cut_count, share, TILE), "cuts", 0, 0)
    total = ring_total(jnp.sum(pieces.astype(F32), axis=0).astype(BF16))
    spread = jnp.broadcast_to(total.astype(BF16)[None], (cut_count, share, TILE))
    mine = lax.all_to_all(spread, "cuts", 0, 0).reshape(HALF, TILE, TILE)
    other = exchange(mine)
    (corrected,) = call(
        functools.partial(correct_kernel, rows_all),
        [shape((rows_mine, columns))],
        [pair],
        [field, mine, other],
        [
            VMEM((PAIRS + 1, TILE, TILE), BF16),
            VMEM((tiles, rows_mine, TILE), BF16),
            VMEM((tiles, TILE), F32),
        ],
        1 << 29,
    )
    return corrected


def solution(mesh):
    return jax.shard_map(
        body,
        mesh=mesh,
        in_specs=(P("row", None, None, None), P("row", None), P(), P(), P(("row", "cuts"), None)),
        out_specs=P(("row", "cuts"), None),
        check_vma=False,
    )
```

```python
import functools

import jax
import jax.numpy as jnp
from jax import lax
from jax.experimental import pallas as pl
from jax.experimental.pallas import tpu as pltpu
from jax.sharding import PartitionSpec as P

HB = 8
BS = 128
NINT = 8
TILE = 128
PAIRS = 42
HALF = PAIRS // 2
FLIGHT = 4
REACH = 4
VMEM = pltpu.VMEM
SMEM = pltpu.SMEM
F32 = jnp.float32
BF16 = jnp.bfloat16


def vmem(count):
    return [pl.BlockSpec(memory_space=VMEM)] * count


def smem(count):
    return [pl.BlockSpec(memory_space=SMEM)] * count


def call(kernel, outs, scalars, arrays, scratch=(), flops=0, limit=24 << 20):
    moved = sum(a.size * a.dtype.itemsize for a in (*arrays, *outs))
    return pl.pallas_call(
        kernel,
        out_shape=tuple(outs),
        in_specs=smem(len(scalars)) + vmem(len(arrays)),
        out_specs=tuple(vmem(len(outs))),
        scratch_shapes=list(scratch),
        compiler_params=pltpu.CompilerParams(vmem_limit_bytes=limit),
        cost_estimate=pl.CostEstimate(flops=flops, bytes_accessed=moved, transcendentals=0),
    )(*scalars, *arrays)


def shape(dims, dtype=BF16):
    return jax.ShapeDtypeStruct(dims, dtype)


def table_kernel(where_ref, turned_ref, width_ref, interval_ref, near_ref, far_ref, pair_ref, list_ref):
    slots, blocks = turned_ref.shape
    first, total, cut = where_ref[0], where_ref[1], where_ref[2]
    edge = blocks // 3

    def one_row(b, _):
        line = jnp.where(b < edge, b, b - edge)
        outer = (b < edge) | (b >= 2 * edge)

        @pl.when(outer)
        def _():
            for k in range(edge):
                far_ref[line, k] = edge

        found = jnp.int32(0)
        for n in range(slots):
            away = turned_ref[n, b] - first
            away = jnp.where(away < -HB, away + total, away)
            away = jnp.where(away >= total - HB, away - total, away)
            local = (away >= 0) & (away < blocks)
            near_ref[n, b] = jnp.where(local, away, blocks)
            halo = jnp.where(away < 0, away + HB, away - blocks)

            @pl.when(jnp.logical_not(local))
            def _():
                far_ref[line, found] = n * 16 + halo

            found += jnp.where(local, 0, 1)
        return 0

    lax.fori_loop(0, blocks, one_row, 0)
    tiles = pair_ref.shape[0] // REACH
    ends = []
    end = jnp.int32(0)
    for s in range(width_ref.shape[0]):
        end += width_ref[s] // TILE
        ends.append(end)

    def slice_of(t):
        index = jnp.int32(0)
        for end in ends:
            index += jnp.where(t >= end, 1, 0)
        return index

    lanes = [slice_of(t) for t in range(tiles)]
    slot = jnp.int32(0)
    for m in range(PAIRS + 1):
        list_ref[m] = 0
    for i in range(tiles):
        for d in range(REACH):
            if i + d < tiles:
                valid = lanes[i + d] - lanes[i] <= 1
                pair_ref[i * REACH + d] = jnp.where(valid, slot, PAIRS)
                list_ref[jnp.where(valid, slot, PAIRS)] = i * REACH + d
                slot += jnp.where(valid, 1, 0)
            else:
                pair_ref[i * REACH + d] = PAIRS
    core = where_ref[3]
    pair_ref[tiles * REACH] = core
    near_ref[slots, 0] = core
    near_ref[slots, 1] = interval_ref[slice_of(cut)]
    far_ref[2 * edge, 0] = core


def turn_kernel(start_ref, out_ref, tiles_ref, read, written):
    tiles = out_ref.shape[0]

    def load(t):
        return pltpu.make_async_copy(
            start_ref.at[:, t * TILE : (t + 1) * TILE], tiles_ref.at[t], read.at[t]
        )

    def store(t):
        return pltpu.make_async_copy(tiles_ref.at[t], out_ref.at[t], written.at[t])

    for t in range(tiles):
        load(t).start()
    for t in range(tiles):
        load(t).wait()
        store(t).start()
    for t in range(tiles):
        store(t).wait()


def near_kernel(scale, near_ref, ham_ref, inner_ref, mid_ref, outer_ref, *rest):
    first = scale == 1
    blocks, slots = ham_ref.shape[:2]
    if first:
        mid_out, edge_out, ham_out, stack, loaded = rest
        chunk = blocks // loaded.shape[0]

        def load(c):
            rows = slice(c * chunk, (c + 1) * chunk)
            return pltpu.make_async_copy(ham_ref.at[rows], ham_out.at[rows], loaded.at[c])

        for c in range(FLIGHT):
            load(c).start()
        ham = ham_out
    else:
        mid_out, edge_out, before, stack = rest[-4:]
        ham = ham_ref
    third = blocks // 3
    span = third * BS
    core = near_ref[slots, 0]
    inner_at, outer_at = (1 - core) * 2 * span, core * 2 * span

    def spread(inner, mid, outer, into):
        into[pl.ds(pl.multiple_of(inner_at, span), span)] = inner[...]
        into[pl.ds(pl.multiple_of(outer_at, span), span)] = outer[...]
        into[span : 2 * span] = mid[...]

    spread(inner_ref, mid_ref, outer_ref, stack)
    stack[blocks * BS :] = jnp.zeros((BS, TILE), BF16)
    if not first:
        spread(*rest[:3], before)
    centre = -0.5 + near_ref[slots, 1].astype(F32) * F32(1 / (NINT - 1))

    def tile_at(n, b):
        return stack[pl.ds(pl.multiple_of(near_ref[n, b] * BS, BS), BS), :]

    for b in range(blocks):
        if first and b % chunk == 0:
            c = b // chunk
            load(c).wait()
            if c + FLIGHT < blocks // chunk:
                load(c + FLIGHT).start()
        total = jnp.zeros((BS, TILE), F32)
        for n in range(0, slots, 2):
            if n + 1 < slots:
                left = jnp.concatenate([ham[b, n], ham[b, n + 1]], axis=1)
                right = jnp.concatenate([tile_at(n, b), tile_at(n + 1, b)], axis=0)
            else:
                left, right = ham[b, n], tile_at(n, b)
            total += jnp.dot(left, right, preferred_element_type=F32)
        part = b // third
        here = slice((b - part * third) * BS, (b - part * third + 1) * BS)
        own = stack[b * BS : (b + 1) * BS].astype(F32)
        value = total - centre * own
        if not first:
            value = scale * value - before[b * BS : (b + 1) * BS].astype(F32)
        if part == 1:
            mid_out[here, :] = value.astype(BF16)
        else:
            edge_out[part // 2, here, :] = value


def add_halo(scale, far_ref, ham_ref, stack, edge_ref, side, k, edge):
    index = k + side * (edge - 1 - 2 * k)
    b = k + side * (3 * edge - 1 - 2 * k)
    left, right = [], []
    for slot_at in range(edge - k):
        entry = far_ref[side * edge + index, slot_at]
        slot = entry // 16
        left.append(ham_ref[b, slot])
        start = pl.multiple_of((entry - slot * 16) * BS, BS)
        right.append(stack[pl.ds(start, BS), :])
    here = pl.ds(pl.multiple_of(index * BS, BS), BS)
    total = edge_ref[side, here, :]
    for slot_at in range(0, edge - k, 2):
        lhs = jnp.concatenate(left[slot_at : slot_at + 2], axis=1)
        rhs = jnp.concatenate(right[slot_at : slot_at + 2], axis=0)
        total += scale * jnp.dot(lhs, rhs, preferred_element_type=F32)
    return index, total.astype(BF16)


def edge_kernel(scale, outer, far_ref, ham_ref, halo_ref, edge_ref, out_ref, stack):
    span = halo_ref.shape[0]
    edge = span // BS
    core = far_ref[2 * edge, 0]
    side = core if outer else 1 - core
    stack[:span] = halo_ref[...]
    stack[span:] = jnp.zeros((BS, TILE), BF16)
    for k in range(edge):
        index, value = add_halo(scale, far_ref, ham_ref, stack, edge_ref, side, k, edge)
        out_ref[pl.ds(pl.multiple_of(index * BS, BS), BS), :] = value


def joined_kernel(scale, far_ref, ham_ref, inner_ref, outer_ref, edge_ref, mid_ref, out_ref, stack):
    span = inner_ref.shape[0]
    edge = span // BS
    core = far_ref[2 * edge, 0]
    for side, ref in ((1 - core, inner_ref), (core, outer_ref)):
        stack[side, :span] = ref[...]
        stack[side, span:] = jnp.zeros((BS, TILE), BF16)
    out_ref[span : 2 * span, :] = mid_ref[...]
    for side in range(2):
        for k in range(edge):
            index, value = add_halo(
                scale, far_ref, ham_ref, stack.at[side], edge_ref, side, k, edge
            )
            at = side * 2 * span + index * BS
            out_ref[at : at + BS, :] = value


def gram_kernel(keep, pair_ref, list_ref, field_ref, out_ref, turned):
    tiles = field_ref.shape[0]
    core = pair_ref[tiles * REACH]
    first = (core if keep else 1 - core) * HALF
    for t in range(tiles):
        turned[t] = field_ref[t].T
    for m in range(HALF):
        code = list_ref[first + m]
        low = code // REACH
        high = low + code - low * REACH
        block = jnp.dot(turned[low], field_ref[high], preferred_element_type=F32)
        out_ref[m] = block.astype(out_ref.dtype)


def correct_kernel(rows_all, pair_ref, field_ref, mine_ref, other_ref, out_ref, gram, scaled, norm):
    tiles = field_ref.shape[0]
    core = pair_ref[tiles * REACH]
    gram[pl.ds(core * HALF, HALF)] = mine_ref[...]
    gram[pl.ds(HALF - core * HALF, HALF)] = other_ref[...]
    gram[PAIRS] = jnp.zeros((TILE, TILE), BF16)
    at_row = lax.broadcasted_iota(jnp.int32, (TILE, TILE), 0)
    at_col = lax.broadcasted_iota(jnp.int32, (TILE, TILE), 1)
    eye = at_row == at_col
    for t in range(tiles):
        block = gram[pair_ref[t * REACH]].astype(F32)
        squares = jnp.sum(jnp.where(eye, block, 0.0), axis=0, keepdims=True)
        inverse = lax.rsqrt(squares / rows_all + 1e-05)
        norm[t : t + 1, :] = inverse
        scaled[t] = (field_ref[t].astype(F32) * (inverse * inverse)).astype(BF16)
    for j in range(tiles):
        below = range(max(0, j - REACH + 1), j + 1)
        left = jnp.concatenate([scaled[i] for i in below], axis=1)
        right = jnp.concatenate([gram[pair_ref[i * REACH + j - i]] for i in below], axis=0)
        total = jnp.dot(left, right, preferred_element_type=F32)
        above = range(j + 1, min(tiles, j + REACH))
        if above:
            left = jnp.concatenate([scaled[i] for i in above], axis=1)
            right = jnp.concatenate([gram[pair_ref[j * REACH + i - j]] for i in above], axis=1)
            total += lax.dot_general(
                left, right, (((1,), (1,)), ((), ())), preferred_element_type=F32
            )
        value = norm[j : j + 1, :] * (1.5 * field_ref[j].astype(F32) - (0.5 / rows_all) * total)
        out_ref[:, j * TILE : (j + 1) * TILE] = value.astype(BF16)


def shift(array, chips):
    size = lax.axis_size("row")
    return lax.ppermute(
        array, "row", [(i, (i + 2 * chips * (1 - 2 * (i % 2))) % size) for i in range(size)]
    )


def exchange(array):
    return lax.ppermute(array, "row", [(i, i ^ 1) for i in range(lax.axis_size("row"))])


def swap_outer(array):
    size = lax.axis_size("row")
    return lax.ppermute(array, "row", [(i, (i - 1 + 2 * (i % 2)) % size) for i in range(size)])


def ring_total(piece):
    own = piece.astype(F32)
    pair = own + shift(piece, -1).astype(F32)
    three = pair + shift(piece, 1).astype(F32)
    after = shift(three.astype(BF16), -3).astype(F32)
    before = shift(pair.astype(BF16), 3).astype(F32)
    return three + after + before


def body(ham_blocks, neighbors, slice_widths, interval_index, start_vectors):
    rows_mine, columns = start_vectors.shape
    tiles = columns // TILE
    blocks, slots = ham_blocks.shape[:2]
    row_count = lax.axis_size("row")
    rows_all = blocks * BS * row_count
    panel_rows = blocks * BS
    span = panel_rows // 3
    turned = pl.pallas_call(
        turn_kernel,
        out_shape=shape((tiles, rows_mine, TILE)),
        in_specs=[pl.BlockSpec(memory_space=pltpu.HBM)],
        out_specs=pl.BlockSpec(memory_space=pltpu.HBM),
        scratch_shapes=[
            VMEM((tiles, rows_mine, TILE), BF16),
            pltpu.SemaphoreType.DMA((tiles,)),
            pltpu.SemaphoreType.DMA((tiles,)),
        ],
        compiler_params=pltpu.CompilerParams(vmem_limit_bytes=62 << 20),
    )(start_vectors)
    panel = lax.all_to_all(turned, "cuts", 0, 0).reshape(panel_rows, TILE)

    row = lax.axis_index("row")
    place = jnp.stack(
        [row * blocks, jnp.int32(blocks * row_count), lax.axis_index("cuts"), row % 2]
    ).astype(jnp.int32)
    near, far, pair, listed = pl.pallas_call(
        table_kernel,
        out_shape=(
            shape((slots + 1, blocks), jnp.int32),
            shape((2 * blocks // 3 + 1, HB), jnp.int32),
            shape((tiles * REACH + 1,), jnp.int32),
            shape((PAIRS + 1,), jnp.int32),
        ),
        in_specs=smem(4),
        out_specs=tuple(smem(4)),
        compiler_params=pltpu.CompilerParams(vmem_limit_bytes=1 << 20),
        cost_estimate=pl.CostEstimate(flops=1 << 20, bytes_accessed=1 << 12, transcendentals=0),
    )(place, neighbors.T, slice_widths, interval_index)
    panel, near, far, pair, listed = lax.optimization_barrier((panel, near, far, pair, listed))
    work = 2 * blocks * slots * BS * BS * TILE
    outs = [shape((span, TILE)), shape((2, span, TILE), F32)]
    stacks = [VMEM((panel_rows, TILE), BF16), VMEM((panel_rows + BS, TILE), BF16)]

    def halos(inner, outer):
        from_outer = swap_outer(outer)
        return exchange(inner), from_outer

    def apply_first(field):
        inner, mid, outer = field
        from_inner, from_outer = halos(inner, outer)
        mid, edges, ham = pl.pallas_call(
            functools.partial(near_kernel, 1),
            out_shape=(*outs, shape(ham_blocks.shape)),
            in_specs=smem(1) + [pl.BlockSpec(memory_space=pltpu.HBM)] + vmem(3),
            out_specs=tuple(vmem(3)),
            scratch_shapes=[stacks[1], pltpu.SemaphoreType.DMA((FLIGHT,))],
            compiler_params=pltpu.CompilerParams(vmem_limit_bytes=40 << 20),
            cost_estimate=pl.CostEstimate(
                flops=work, bytes_accessed=ham_blocks.size * 2, transcendentals=0
            ),
        )(near, ham_blocks, inner, mid, outer)
        ham = pltpu.with_memory_space_constraint(ham, VMEM)
        return ham, (from_inner, from_outer, edges, mid)

    def apply_next(ham, field, before):
        inner, mid, outer = field
        from_inner, from_outer = halos(inner, outer)
        mid, edges = call(
            functools.partial(near_kernel, 2),
            outs,
            [near],
            [ham, inner, mid, outer, *before],
            stacks,
            work,
        )
        return from_inner, from_outer, edges, mid

    def edges_of(scale, ham, from_inner, from_outer, edges, mid):
        def side(outer, halo):
            (out,) = call(
                functools.partial(edge_kernel, scale, outer),
                [shape((span, TILE))],
                [far],
                [ham, halo, edges],
                [VMEM((span + BS, TILE), BF16)],
                work // 8,
            )
            return out

        outer = side(True, from_outer)
        return side(False, from_inner), mid, outer

    low, mid, high = (panel[q * span : (q + 1) * span] for q in range(3))
    even = row % 2 == 0
    start = (jnp.where(even, high, low), mid, jnp.where(even, low, high))
    ham, parts = apply_first(start)
    first = edges_of(1, ham, *parts)
    second = edges_of(2, ham, *apply_next(ham, first, start))
    from_inner, from_outer, edges, mid = apply_next(ham, second, first)
    (filtered,) = call(
        functools.partial(joined_kernel, 2),
        [shape((panel_rows, TILE))],
        [far],
        [ham, from_inner, from_outer, edges, mid],
        [VMEM((2, span + BS, TILE), BF16)],
        work // 4,
    )

    field = lax.all_to_all(filtered.reshape(tiles, rows_mine, TILE), "cuts", 0, 0)

    def gram(keep):
        (out,) = call(
            functools.partial(gram_kernel, keep),
            [shape((HALF, TILE, TILE), F32 if keep else BF16)],
            [pair, listed],
            [field],
            [VMEM((tiles, TILE, rows_mine), BF16)],
            1 << 28,
        )
        return out

    partial = (gram(True) + exchange(gram(False)).astype(F32)).astype(BF16)
    cut_count = lax.axis_size("cuts")
    share = HALF * TILE // cut_count
    pieces = lax.all_to_all(partial.reshape(cut_count, share, TILE), "cuts", 0, 0)
    total = ring_total(jnp.sum(pieces.astype(F32), axis=0).astype(BF16))
    spread = jnp.broadcast_to(total.astype(BF16)[None], (cut_count, share, TILE))
    mine = lax.all_to_all(spread, "cuts", 0, 0).reshape(HALF, TILE, TILE)
    other = exchange(mine)
    (corrected,) = call(
        functools.partial(correct_kernel, rows_all),
        [shape((rows_mine, columns))],
        [pair],
        [field, mine, other],
        [
            VMEM((PAIRS + 1, TILE, TILE), BF16),
            VMEM((tiles, rows_mine, TILE), BF16),
            VMEM((tiles, TILE), F32),
        ],
        1 << 29,
    )
    return corrected


def solution(mesh):
    return jax.shard_map(
        body,
        mesh=mesh,
        in_specs=(P("row", None, None, None), P("row", None), P(), P(), P(("row", "cuts"), None)),
        out_specs=P(("row", "cuts"), None),
        check_vma=False,
    )
```

```python
import functools

import jax
import jax.numpy as jnp
from jax import lax
from jax.experimental import pallas as pl
from jax.experimental.pallas import tpu as pltpu
from jax.sharding import PartitionSpec as P

HB = 8
BS = 128
NINT = 8
TILE = 128
SIDE = 13
DIAG = 4
HALF = DIAG + 1 + SIDE
ZERO = 2 * HALF
FLIGHT = 4
REACH = 4
VMEM = pltpu.VMEM
SMEM = pltpu.SMEM
F32 = jnp.float32
BF16 = jnp.bfloat16


def vmem(count):
    return [pl.BlockSpec(memory_space=VMEM)] * count


def smem(count):
    return [pl.BlockSpec(memory_space=SMEM)] * count


def call(kernel, outs, scalars, arrays, scratch=(), flops=0, limit=24 << 20):
    moved = sum(a.size * a.dtype.itemsize for a in (*arrays, *outs))
    return pl.pallas_call(
        kernel,
        out_shape=tuple(outs),
        in_specs=smem(len(scalars)) + vmem(len(arrays)),
        out_specs=tuple(vmem(len(outs))),
        scratch_shapes=list(scratch),
        compiler_params=pltpu.CompilerParams(vmem_limit_bytes=limit),
        cost_estimate=pl.CostEstimate(flops=flops, bytes_accessed=moved, transcendentals=0),
    )(*scalars, *arrays)


def shape(dims, dtype=BF16):
    return jax.ShapeDtypeStruct(dims, dtype)


def table_kernel(where_ref, turned_ref, width_ref, interval_ref, near_ref, far_ref, pair_ref, list_ref):
    slots, blocks = turned_ref.shape
    first, total, cut = where_ref[0], where_ref[1], where_ref[2]
    edge = blocks // 3

    def one_row(b, _):
        line = jnp.where(b < edge, b, b - edge)
        outer = (b < edge) | (b >= 2 * edge)

        @pl.when(outer)
        def _():
            for k in range(edge):
                far_ref[line, k] = edge

        found = jnp.int32(0)
        for n in range(slots):
            away = turned_ref[n, b] - first
            away = jnp.where(away < -HB, away + total, away)
            away = jnp.where(away >= total - HB, away - total, away)
            local = (away >= 0) & (away < blocks)
            near_ref[n, b] = jnp.where(local, away, blocks)
            halo = jnp.where(away < 0, away + HB, away - blocks)

            @pl.when(jnp.logical_not(local))
            def _():
                far_ref[line, found] = n * 16 + halo

            found += jnp.where(local, 0, 1)
        return 0

    lax.fori_loop(0, blocks, one_row, 0)
    tiles = pair_ref.shape[0] // REACH
    ends = []
    end = jnp.int32(0)
    for s in range(width_ref.shape[0]):
        end += width_ref[s] // TILE
        ends.append(end)

    def slice_of(t):
        index = jnp.int32(0)
        for end in ends:
            index += jnp.where(t >= end, 1, 0)
        return index

    lanes = [slice_of(t) for t in range(tiles)]
    found = jnp.int32(0)
    for m in range(2 * SIDE + 1):
        list_ref[m] = 1
    for i in range(tiles):
        for d in range(1, REACH):
            if i + d < tiles:
                valid = lanes[i + d] - lanes[i] <= 1
                slot = found + DIAG + 1 + jnp.where(found >= SIDE, DIAG + 1, 0)
                pair_ref[i * REACH + d] = jnp.where(valid, slot, ZERO)
                list_ref[jnp.where(valid, found, 2 * SIDE)] = i * REACH + d
                found += jnp.where(valid, 1, 0)
    core = where_ref[3]
    pair_ref[tiles * REACH] = core
    near_ref[slots, 0] = core
    near_ref[slots, 1] = interval_ref[slice_of(cut)]
    far_ref[2 * edge, 0] = core


def turn_kernel(start_ref, out_ref, tiles_ref, read, written):
    tiles = out_ref.shape[0]

    def load(t):
        return pltpu.make_async_copy(
            start_ref.at[:, t * TILE : (t + 1) * TILE], tiles_ref.at[t], read.at[t]
        )

    def store(t):
        return pltpu.make_async_copy(tiles_ref.at[t], out_ref.at[t], written.at[t])

    for t in range(tiles):
        load(t).start()
    for t in range(tiles):
        load(t).wait()
        store(t).start()
    for t in range(tiles):
        store(t).wait()


def near_kernel(scale, near_ref, ham_ref, inner_ref, mid_ref, outer_ref, *rest):
    first = scale == 1
    blocks, slots = ham_ref.shape[:2]
    if first:
        mid_out, edge_out, ham_out, stack, loaded = rest
        chunk = blocks // loaded.shape[0]

        def load(c):
            rows = slice(c * chunk, (c + 1) * chunk)
            return pltpu.make_async_copy(ham_ref.at[rows], ham_out.at[rows], loaded.at[c])

        for c in range(FLIGHT):
            load(c).start()
        ham = ham_out
    else:
        mid_out, edge_out, before, stack = rest[-4:]
        ham = ham_ref
    third = blocks // 3
    span = third * BS
    core = near_ref[slots, 0]
    inner_at, outer_at = (1 - core) * 2 * span, core * 2 * span

    def spread(inner, mid, outer, into):
        into[pl.ds(pl.multiple_of(inner_at, span), span)] = inner[...]
        into[pl.ds(pl.multiple_of(outer_at, span), span)] = outer[...]
        into[span : 2 * span] = mid[...]

    spread(inner_ref, mid_ref, outer_ref, stack)
    stack[blocks * BS :] = jnp.zeros((BS, TILE), BF16)
    if not first:
        spread(*rest[:3], before)
    centre = -0.5 + near_ref[slots, 1].astype(F32) * F32(1 / (NINT - 1))

    def tile_at(n, b):
        return stack[pl.ds(pl.multiple_of(near_ref[n, b] * BS, BS), BS), :]

    for b in range(blocks):
        if first and b % chunk == 0:
            c = b // chunk
            load(c).wait()
            if c + FLIGHT < blocks // chunk:
                load(c + FLIGHT).start()
        total = jnp.zeros((BS, TILE), F32)
        for n in range(0, slots, 2):
            if n + 1 < slots:
                left = jnp.concatenate([ham[b, n], ham[b, n + 1]], axis=1)
                right = jnp.concatenate([tile_at(n, b), tile_at(n + 1, b)], axis=0)
            else:
                left, right = ham[b, n], tile_at(n, b)
            total += jnp.dot(left, right, preferred_element_type=F32)
        part = b // third
        here = slice((b - part * third) * BS, (b - part * third + 1) * BS)
        own = stack[b * BS : (b + 1) * BS].astype(F32)
        value = total - centre * own
        if not first:
            value = scale * value - before[b * BS : (b + 1) * BS].astype(F32)
        if part == 1:
            mid_out[here, :] = value.astype(BF16)
        else:
            edge_out[part // 2, here, :] = value


def add_halo(scale, far_ref, ham_ref, stack, edge_ref, side, k, edge):
    index = k + side * (edge - 1 - 2 * k)
    b = k + side * (3 * edge - 1 - 2 * k)
    left, right = [], []
    for slot_at in range(edge - k):
        entry = far_ref[side * edge + index, slot_at]
        slot = entry // 16
        left.append(ham_ref[b, slot])
        start = pl.multiple_of((entry - slot * 16) * BS, BS)
        right.append(stack[pl.ds(start, BS), :])
    here = pl.ds(pl.multiple_of(index * BS, BS), BS)
    total = edge_ref[side, here, :]
    for slot_at in range(0, edge - k, 2):
        lhs = jnp.concatenate(left[slot_at : slot_at + 2], axis=1)
        rhs = jnp.concatenate(right[slot_at : slot_at + 2], axis=0)
        total += scale * jnp.dot(lhs, rhs, preferred_element_type=F32)
    return index, total.astype(BF16)


def edge_kernel(scale, outer, far_ref, ham_ref, halo_ref, edge_ref, out_ref, stack):
    span = halo_ref.shape[0]
    edge = span // BS
    core = far_ref[2 * edge, 0]
    side = core if outer else 1 - core
    stack[:span] = halo_ref[...]
    stack[span:] = jnp.zeros((BS, TILE), BF16)
    for k in range(edge):
        index, value = add_halo(scale, far_ref, ham_ref, stack, edge_ref, side, k, edge)
        out_ref[pl.ds(pl.multiple_of(index * BS, BS), BS), :] = value


def joined_kernel(scale, far_ref, ham_ref, inner_ref, outer_ref, edge_ref, mid_ref, out_ref, stack):
    span = inner_ref.shape[0]
    edge = span // BS
    core = far_ref[2 * edge, 0]
    for side, ref in ((1 - core, inner_ref), (core, outer_ref)):
        stack[side, :span] = ref[...]
        stack[side, span:] = jnp.zeros((BS, TILE), BF16)
    out_ref[span : 2 * span, :] = mid_ref[...]
    for side in range(2):
        for k in range(edge):
            index, value = add_halo(
                scale, far_ref, ham_ref, stack.at[side], edge_ref, side, k, edge
            )
            at = side * 2 * span + index * BS
            out_ref[at : at + BS, :] = value


def places():
    at_row = lax.broadcasted_iota(jnp.int32, (TILE, TILE), 0)
    at_col = lax.broadcasted_iota(jnp.int32, (TILE, TILE), 1)
    return at_row, at_col


def gram_kernel(keep, pair_ref, list_ref, field_ref, out_ref, turned):
    tiles = field_ref.shape[0]
    core = pair_ref[tiles * REACH]
    half = core if keep else 1 - core
    at_row, at_col = places()
    for t in range(tiles):
        turned[t] = field_ref[t].T

    def block(low, high):
        return jnp.dot(turned[low], field_ref[high], preferred_element_type=F32)

    extra = jnp.zeros((TILE, TILE), F32)
    for k in range(DIAG):
        tile = (half * DIAG + k) * 2
        upper = block(tile, tile)
        lower = block(tile + 1, tile + 1)
        squares = jnp.sum(jnp.where(at_row == at_col, lower, 0.0), axis=0, keepdims=True)
        extra = jnp.where(at_row == k, squares, extra)
        out_ref[k] = jnp.where(at_row <= at_col, upper, lower).astype(out_ref.dtype)
    out_ref[DIAG] = extra.astype(out_ref.dtype)
    for m in range(SIDE):
        code = list_ref[half * SIDE + m]
        low = code // REACH
        high = low + code - low * REACH
        out_ref[DIAG + 1 + m] = block(low, high).astype(out_ref.dtype)


def correct_kernel(rows_all, pair_ref, field_ref, mine_ref, other_ref, out_ref, gram, own, scaled, norm):
    tiles = field_ref.shape[0]
    core = pair_ref[tiles * REACH]
    gram[pl.ds(core * HALF, HALF)] = mine_ref[...]
    gram[pl.ds(HALF - core * HALF, HALF)] = other_ref[...]
    gram[ZERO] = jnp.zeros((TILE, TILE), BF16)
    at_row, at_col = places()

    def prepare(t, block, squares):
        own[t] = block.astype(BF16)
        inverse = lax.rsqrt(squares / rows_all + 1e-05)
        norm[t : t + 1, :] = inverse
        scaled[t] = (field_ref[t].astype(F32) * (inverse * inverse)).astype(BF16)

    for q in range(tiles // 2):
        half, k = q // DIAG, q % DIAG
        packed = gram[half * HALF + k].astype(F32)
        flipped = packed.T
        upper = jnp.where(at_row <= at_col, packed, flipped)
        squares = jnp.sum(jnp.where(at_row == at_col, packed, 0.0), axis=0, keepdims=True)
        prepare(2 * q, upper, squares)
        squares = gram[half * HALF + DIAG].astype(F32)[k : k + 1, :]
        lower = jnp.where(at_row > at_col, packed, flipped)
        prepare(2 * q + 1, jnp.where(at_row == at_col, squares, lower), squares)
    for j in range(tiles):
        below = range(max(0, j - REACH + 1), j)
        left = jnp.concatenate([scaled[i] for i in below] + [scaled[j]], axis=1)
        right = jnp.concatenate(
            [gram[pair_ref[i * REACH + j - i]] for i in below] + [own[j]], axis=0
        )
        total = jnp.dot(left, right, preferred_element_type=F32)
        above = range(j + 1, min(tiles, j + REACH))
        if above:
            left = jnp.concatenate([scaled[i] for i in above], axis=1)
            right = jnp.concatenate([gram[pair_ref[j * REACH + i - j]] for i in above], axis=1)
            total += lax.dot_general(
                left, right, (((1,), (1,)), ((), ())), preferred_element_type=F32
            )
        value = norm[j : j + 1, :] * (1.5 * field_ref[j].astype(F32) - (0.5 / rows_all) * total)
        out_ref[:, j * TILE : (j + 1) * TILE] = value.astype(BF16)


def shift(array, chips):
    size = lax.axis_size("row")
    return lax.ppermute(
        array, "row", [(i, (i + 2 * chips * (1 - 2 * (i % 2))) % size) for i in range(size)]
    )


def exchange(array):
    return lax.ppermute(array, "row", [(i, i ^ 1) for i in range(lax.axis_size("row"))])


def swap_outer(array):
    size = lax.axis_size("row")
    return lax.ppermute(array, "row", [(i, (i - 1 + 2 * (i % 2)) % size) for i in range(size)])


def ring_total(piece):
    own = piece.astype(F32)
    pair = own + shift(piece, -1).astype(F32)
    three = pair + shift(piece, 1).astype(F32)
    after = shift(three.astype(BF16), -3).astype(F32)
    before = shift(pair.astype(BF16), 3).astype(F32)
    return three + after + before


def body(ham_blocks, neighbors, slice_widths, interval_index, start_vectors):
    rows_mine, columns = start_vectors.shape
    tiles = columns // TILE
    blocks, slots = ham_blocks.shape[:2]
    row_count = lax.axis_size("row")
    rows_all = blocks * BS * row_count
    panel_rows = blocks * BS
    span = panel_rows // 3
    turned = pl.pallas_call(
        turn_kernel,
        out_shape=shape((tiles, rows_mine, TILE)),
        in_specs=[pl.BlockSpec(memory_space=pltpu.HBM)],
        out_specs=pl.BlockSpec(memory_space=pltpu.HBM),
        scratch_shapes=[
            VMEM((tiles, rows_mine, TILE), BF16),
            pltpu.SemaphoreType.DMA((tiles,)),
            pltpu.SemaphoreType.DMA((tiles,)),
        ],
        compiler_params=pltpu.CompilerParams(vmem_limit_bytes=62 << 20),
    )(start_vectors)
    panel = lax.all_to_all(turned, "cuts", 0, 0).reshape(panel_rows, TILE)

    row = lax.axis_index("row")
    place = jnp.stack(
        [row * blocks, jnp.int32(blocks * row_count), lax.axis_index("cuts"), row % 2]
    ).astype(jnp.int32)
    near, far, pair, listed = pl.pallas_call(
        table_kernel,
        out_shape=(
            shape((slots + 1, blocks), jnp.int32),
            shape((2 * blocks // 3 + 1, HB), jnp.int32),
            shape((tiles * REACH + 1,), jnp.int32),
            shape((2 * SIDE + 1,), jnp.int32),
        ),
        in_specs=smem(4),
        out_specs=tuple(smem(4)),
        compiler_params=pltpu.CompilerParams(vmem_limit_bytes=1 << 20),
        cost_estimate=pl.CostEstimate(flops=1 << 20, bytes_accessed=1 << 12, transcendentals=0),
    )(place, neighbors.T, slice_widths, interval_index)
    panel, near, far, pair, listed = lax.optimization_barrier((panel, near, far, pair, listed))
    work = 2 * blocks * slots * BS * BS * TILE
    outs = [shape((span, TILE)), shape((2, span, TILE), F32)]
    stacks = [VMEM((panel_rows, TILE), BF16), VMEM((panel_rows + BS, TILE), BF16)]

    def halos(inner, outer):
        from_outer = swap_outer(outer)
        return exchange(inner), from_outer

    def apply_first(field):
        inner, mid, outer = field
        from_inner, from_outer = halos(inner, outer)
        mid, edges, ham = pl.pallas_call(
            functools.partial(near_kernel, 1),
            out_shape=(*outs, shape(ham_blocks.shape)),
            in_specs=smem(1) + [pl.BlockSpec(memory_space=pltpu.HBM)] + vmem(3),
            out_specs=tuple(vmem(3)),
            scratch_shapes=[stacks[1], pltpu.SemaphoreType.DMA((FLIGHT,))],
            compiler_params=pltpu.CompilerParams(vmem_limit_bytes=40 << 20),
            cost_estimate=pl.CostEstimate(
                flops=work, bytes_accessed=ham_blocks.size * 2, transcendentals=0
            ),
        )(near, ham_blocks, inner, mid, outer)
        ham = pltpu.with_memory_space_constraint(ham, VMEM)
        return ham, (from_inner, from_outer, edges, mid)

    def apply_next(ham, field, before):
        inner, mid, outer = field
        from_inner, from_outer = halos(inner, outer)
        mid, edges = call(
            functools.partial(near_kernel, 2),
            outs,
            [near],
            [ham, inner, mid, outer, *before],
            stacks,
            work,
        )
        return from_inner, from_outer, edges, mid

    def edges_of(scale, ham, from_inner, from_outer, edges, mid):
        def side(outer, halo):
            (out,) = call(
                functools.partial(edge_kernel, scale, outer),
                [shape((span, TILE))],
                [far],
                [ham, halo, edges],
                [VMEM((span + BS, TILE), BF16)],
                work // 8,
            )
            return out

        outer = side(True, from_outer)
        return side(False, from_inner), mid, outer

    low, mid, high = (panel[q * span : (q + 1) * span] for q in range(3))
    even = row % 2 == 0
    start = (jnp.where(even, high, low), mid, jnp.where(even, low, high))
    ham, parts = apply_first(start)
    first = edges_of(1, ham, *parts)
    second = edges_of(2, ham, *apply_next(ham, first, start))
    from_inner, from_outer, edges, mid = apply_next(ham, second, first)
    (filtered,) = call(
        functools.partial(joined_kernel, 2),
        [shape((panel_rows, TILE))],
        [far],
        [ham, from_inner, from_outer, edges, mid],
        [VMEM((2, span + BS, TILE), BF16)],
        work // 4,
    )

    field = lax.all_to_all(filtered.reshape(tiles, rows_mine, TILE), "cuts", 0, 0)

    def gram(keep):
        (out,) = call(
            functools.partial(gram_kernel, keep),
            [shape((HALF, TILE, TILE), F32 if keep else BF16)],
            [pair, listed],
            [field],
            [VMEM((tiles, TILE, rows_mine), BF16)],
            1 << 28,
        )
        return out

    partial = (gram(True) + exchange(gram(False)).astype(F32)).astype(BF16)
    cut_count = lax.axis_size("cuts")
    share = HALF * TILE // cut_count
    pieces = lax.all_to_all(partial.reshape(cut_count, share, TILE), "cuts", 0, 0)
    total = ring_total(jnp.sum(pieces.astype(F32), axis=0).astype(BF16))
    spread = jnp.broadcast_to(total.astype(BF16)[None], (cut_count, share, TILE))
    mine = lax.all_to_all(spread, "cuts", 0, 0).reshape(HALF, TILE, TILE)
    other = exchange(mine)
    (corrected,) = call(
        functools.partial(correct_kernel, rows_all),
        [shape((rows_mine, columns))],
        [pair],
        [field, mine, other],
        [
            VMEM((2 * HALF + 1, TILE, TILE), BF16),
            VMEM((tiles, TILE, TILE), BF16),
            VMEM((tiles, rows_mine, TILE), BF16),
            VMEM((tiles, TILE), F32),
        ],
        1 << 29,
    )
    return corrected


def solution(mesh):
    return jax.shard_map(
        body,
        mesh=mesh,
        in_specs=(P("row", None, None, None), P("row", None), P(), P(), P(("row", "cuts"), None)),
        out_specs=P(("row", "cuts"), None),
        check_vma=False,
    )
```

```python
import functools

import jax
import jax.numpy as jnp
from jax import lax
from jax.experimental import pallas as pl
from jax.experimental.pallas import tpu as pltpu
from jax.sharding import PartitionSpec as P

HB = 8
BS = 128
NINT = 8
TILE = 128
SIDE = 13
DIAG = 4
HALF = DIAG + 1 + SIDE
ZERO = 2 * HALF
LISTED = 63
FLIGHT = 4
REACH = 4
VMEM = pltpu.VMEM
SMEM = pltpu.SMEM
F32 = jnp.float32
BF16 = jnp.bfloat16


def vmem(count):
    return [pl.BlockSpec(memory_space=VMEM)] * count


def smem(count):
    return [pl.BlockSpec(memory_space=SMEM)] * count


def call(kernel, outs, scalars, arrays, scratch=(), flops=0, limit=24 << 20):
    moved = sum(a.size * a.dtype.itemsize for a in (*arrays, *outs))
    return pl.pallas_call(
        kernel,
        out_shape=tuple(outs),
        in_specs=smem(len(scalars)) + vmem(len(arrays)),
        out_specs=tuple(vmem(len(outs))),
        scratch_shapes=list(scratch),
        compiler_params=pltpu.CompilerParams(vmem_limit_bytes=limit),
        cost_estimate=pl.CostEstimate(flops=flops, bytes_accessed=moved, transcendentals=0),
    )(*scalars, *arrays)


def shape(dims, dtype=BF16):
    return jax.ShapeDtypeStruct(dims, dtype)


def table_kernel(where_ref, turned_ref, width_ref, interval_ref, near_ref, far_ref, pair_ref):
    slots, blocks = turned_ref.shape
    first, total, cut = where_ref[0], where_ref[1], where_ref[2]
    edge = blocks // 3

    def one_row(b, _):
        line = jnp.where(b < edge, b, b - edge)
        outer = (b < edge) | (b >= 2 * edge)

        @pl.when(outer)
        def _():
            for k in range(edge):
                far_ref[line * HB + k] = edge

        found = jnp.int32(0)
        for n in range(slots):
            away = turned_ref[n, b] - first
            away = jnp.where(away < -HB, away + total, away)
            away = jnp.where(away >= total - HB, away - total, away)
            local = (away >= 0) & (away < blocks)
            near_ref[n * blocks + b] = jnp.where(local, away, blocks)
            halo = jnp.where(away < 0, away + HB, away - blocks)

            @pl.when(jnp.logical_not(local))
            def _():
                far_ref[line * HB + found] = n * 16 + halo

            found += jnp.where(local, 0, 1)
        return 0

    lax.fori_loop(0, blocks, one_row, 0)
    tiles = (pair_ref.shape[0] - LISTED) // REACH
    listed = tiles * REACH + 1
    ends = []
    end = jnp.int32(0)
    for s in range(width_ref.shape[0]):
        end += width_ref[s] // TILE
        ends.append(end)

    def slice_of(t):
        index = jnp.int32(0)
        for end in ends:
            index += jnp.where(t >= end, 1, 0)
        return index

    lanes = [slice_of(t) for t in range(tiles)]
    found = jnp.int32(0)
    for m in range(2 * SIDE + 1):
        pair_ref[listed + m] = 1
    for i in range(tiles):
        for d in range(1, REACH):
            if i + d < tiles:
                valid = lanes[i + d] - lanes[i] <= 1
                slot = found + DIAG + 1 + jnp.where(found >= SIDE, DIAG + 1, 0)
                pair_ref[i * REACH + d] = jnp.where(valid, slot, ZERO)
                pair_ref[listed + jnp.where(valid, found, 2 * SIDE)] = i * REACH + d
                found += jnp.where(valid, 1, 0)
    core = where_ref[3]
    pair_ref[tiles * REACH] = core
    near_ref[slots * blocks] = core
    near_ref[slots * blocks + 1] = interval_ref[slice_of(cut)]
    far_ref[2 * edge * HB] = core


def turn_kernel(start_ref, out_ref, tiles_ref, read, written):
    tiles = out_ref.shape[0]

    def load(t):
        return pltpu.make_async_copy(
            start_ref.at[:, t * TILE : (t + 1) * TILE], tiles_ref.at[t], read.at[t]
        )

    def store(t):
        return pltpu.make_async_copy(tiles_ref.at[t], out_ref.at[t], written.at[t])

    for t in range(tiles):
        load(t).start()
    for t in range(tiles):
        load(t).wait()
        store(t).start()
    for t in range(tiles):
        store(t).wait()


def near_kernel(scale, near_ref, ham_ref, inner_ref, mid_ref, outer_ref, *rest):
    first = scale == 1
    blocks, slots = ham_ref.shape[:2]
    if first:
        mid_out, edge_out, ham_out, stack, loaded = rest
        chunk = blocks // loaded.shape[0]

        def load(c):
            rows = slice(c * chunk, (c + 1) * chunk)
            return pltpu.make_async_copy(ham_ref.at[rows], ham_out.at[rows], loaded.at[c])

        for c in range(FLIGHT):
            load(c).start()
        ham = ham_out
    else:
        mid_out, edge_out, before, stack = rest[-4:]
        ham = ham_ref
    third = blocks // 3
    span = third * BS
    core = near_ref[slots * blocks]
    inner_at, outer_at = (1 - core) * 2 * span, core * 2 * span

    def spread(inner, mid, outer, into):
        into[pl.ds(pl.multiple_of(inner_at, span), span)] = inner[...]
        into[pl.ds(pl.multiple_of(outer_at, span), span)] = outer[...]
        into[span : 2 * span] = mid[...]

    spread(inner_ref, mid_ref, outer_ref, stack)
    stack[blocks * BS :] = jnp.zeros((BS, TILE), BF16)
    if not first:
        spread(*rest[:3], before)
    centre = -0.5 + near_ref[slots * blocks + 1].astype(F32) * F32(1 / (NINT - 1))

    def tile_at(n, b):
        return stack[pl.ds(pl.multiple_of(near_ref[n * blocks + b] * BS, BS), BS), :]

    for b in range(blocks):
        if first and b % chunk == 0:
            c = b // chunk
            load(c).wait()
            if c + FLIGHT < blocks // chunk:
                load(c + FLIGHT).start()
        total = jnp.zeros((BS, TILE), F32)
        for n in range(0, slots, 2):
            if n + 1 < slots:
                left = jnp.concatenate([ham[b, n], ham[b, n + 1]], axis=1)
                right = jnp.concatenate([tile_at(n, b), tile_at(n + 1, b)], axis=0)
            else:
                left, right = ham[b, n], tile_at(n, b)
            total += jnp.dot(left, right, preferred_element_type=F32)
        part = b // third
        here = slice((b - part * third) * BS, (b - part * third + 1) * BS)
        own = stack[b * BS : (b + 1) * BS].astype(F32)
        value = total - centre * own
        if not first:
            value = scale * value - before[b * BS : (b + 1) * BS].astype(F32)
        if part == 1:
            mid_out[here, :] = value.astype(BF16)
        else:
            edge_out[part // 2, here, :] = value


def add_halo(scale, far_ref, ham_ref, stack, edge_ref, side, k, edge):
    index = k + side * (edge - 1 - 2 * k)
    b = k + side * (3 * edge - 1 - 2 * k)
    left, right = [], []
    for slot_at in range(edge - k):
        entry = far_ref[(side * edge + index) * HB + slot_at]
        slot = entry // 16
        left.append(ham_ref[b, slot])
        start = pl.multiple_of((entry - slot * 16) * BS, BS)
        right.append(stack[pl.ds(start, BS), :])
    here = pl.ds(pl.multiple_of(index * BS, BS), BS)
    total = edge_ref[side, here, :]
    for slot_at in range(0, edge - k, 2):
        lhs = jnp.concatenate(left[slot_at : slot_at + 2], axis=1)
        rhs = jnp.concatenate(right[slot_at : slot_at + 2], axis=0)
        total += scale * jnp.dot(lhs, rhs, preferred_element_type=F32)
    return index, total.astype(BF16)


def edge_kernel(scale, outer, far_ref, ham_ref, halo_ref, edge_ref, out_ref, stack):
    span = halo_ref.shape[0]
    edge = span // BS
    core = far_ref[2 * edge * HB]
    side = core if outer else 1 - core
    stack[:span] = halo_ref[...]
    stack[span:] = jnp.zeros((BS, TILE), BF16)
    for k in range(edge):
        index, value = add_halo(scale, far_ref, ham_ref, stack, edge_ref, side, k, edge)
        out_ref[pl.ds(pl.multiple_of(index * BS, BS), BS), :] = value


def joined_kernel(scale, far_ref, ham_ref, inner_ref, outer_ref, edge_ref, mid_ref, out_ref, stack):
    span = inner_ref.shape[0]
    edge = span // BS
    core = far_ref[2 * edge * HB]
    for side, ref in ((1 - core, inner_ref), (core, outer_ref)):
        stack[side, :span] = ref[...]
        stack[side, span:] = jnp.zeros((BS, TILE), BF16)
    out_ref[span : 2 * span, :] = mid_ref[...]
    for side in range(2):
        for k in range(edge):
            index, value = add_halo(
                scale, far_ref, ham_ref, stack.at[side], edge_ref, side, k, edge
            )
            at = side * 2 * span + index * BS
            out_ref[at : at + BS, :] = value


def places():
    at_row = lax.broadcasted_iota(jnp.int32, (TILE, TILE), 0)
    at_col = lax.broadcasted_iota(jnp.int32, (TILE, TILE), 1)
    return at_row, at_col


def gram_kernel(keep, table_ref, field_ref, out_ref, turned, pair_ref, fetched):
    tiles = field_ref.shape[0]
    fetch = pltpu.make_async_copy(table_ref, pair_ref, fetched.at[0])
    fetch.start()
    at_row, at_col = places()
    for t in range(tiles):
        turned[t] = field_ref[t].T
    fetch.wait()
    core = pair_ref[tiles * REACH]
    half = core if keep else 1 - core

    def block(low, high):
        return jnp.dot(turned[low], field_ref[high], preferred_element_type=F32)

    extra = jnp.zeros((TILE, TILE), F32)
    for k in range(DIAG):
        tile = (half * DIAG + k) * 2
        upper = block(tile, tile)
        lower = block(tile + 1, tile + 1)
        squares = jnp.sum(jnp.where(at_row == at_col, lower, 0.0), axis=0, keepdims=True)
        extra = jnp.where(at_row == k, squares, extra)
        out_ref[k] = jnp.where(at_row <= at_col, upper, lower).astype(out_ref.dtype)
    out_ref[DIAG] = extra.astype(out_ref.dtype)
    for m in range(SIDE):
        code = pair_ref[tiles * REACH + 1 + half * SIDE + m]
        low = code // REACH
        high = low + code - low * REACH
        out_ref[DIAG + 1 + m] = block(low, high).astype(out_ref.dtype)


def correct_kernel(rows_all, pair_ref, field_ref, mine_ref, other_ref, out_ref, gram, own, scaled, norm):
    tiles = field_ref.shape[0]
    core = pair_ref[tiles * REACH]
    gram[pl.ds(core * HALF, HALF)] = mine_ref[...]
    gram[pl.ds(HALF - core * HALF, HALF)] = other_ref[...]
    gram[ZERO] = jnp.zeros((TILE, TILE), BF16)
    at_row, at_col = places()

    def prepare(t, block, squares):
        own[t] = block.astype(BF16)
        inverse = lax.rsqrt(squares / rows_all + 1e-05)
        norm[t : t + 1, :] = inverse
        scaled[t] = (field_ref[t].astype(F32) * (inverse * inverse)).astype(BF16)

    for q in range(tiles // 2):
        half, k = q // DIAG, q % DIAG
        packed = gram[half * HALF + k].astype(F32)
        flipped = packed.T
        upper = jnp.where(at_row <= at_col, packed, flipped)
        squares = jnp.sum(jnp.where(at_row == at_col, packed, 0.0), axis=0, keepdims=True)
        prepare(2 * q, upper, squares)
        squares = gram[half * HALF + DIAG].astype(F32)[k : k + 1, :]
        lower = jnp.where(at_row > at_col, packed, flipped)
        prepare(2 * q + 1, jnp.where(at_row == at_col, squares, lower), squares)
    for j in range(tiles):
        below = range(max(0, j - REACH + 1), j)
        left = jnp.concatenate([scaled[i] for i in below] + [scaled[j]], axis=1)
        right = jnp.concatenate(
            [gram[pair_ref[i * REACH + j - i]] for i in below] + [own[j]], axis=0
        )
        total = jnp.dot(left, right, preferred_element_type=F32)
        above = range(j + 1, min(tiles, j + REACH))
        if above:
            left = jnp.concatenate([scaled[i] for i in above], axis=1)
            right = jnp.concatenate([gram[pair_ref[j * REACH + i - j]] for i in above], axis=1)
            total += lax.dot_general(
                left, right, (((1,), (1,)), ((), ())), preferred_element_type=F32
            )
        value = norm[j : j + 1, :] * (1.5 * field_ref[j].astype(F32) - (0.5 / rows_all) * total)
        out_ref[:, j * TILE : (j + 1) * TILE] = value.astype(BF16)


def shift(array, chips):
    size = lax.axis_size("row")
    return lax.ppermute(
        array, "row", [(i, (i + 2 * chips * (1 - 2 * (i % 2))) % size) for i in range(size)]
    )


def exchange(array):
    return lax.ppermute(array, "row", [(i, i ^ 1) for i in range(lax.axis_size("row"))])


def swap_outer(array):
    size = lax.axis_size("row")
    return lax.ppermute(array, "row", [(i, (i - 1 + 2 * (i % 2)) % size) for i in range(size)])


def ring_total(piece):
    own = piece.astype(F32)
    pair = own + shift(piece, -1).astype(F32)
    three = pair + shift(piece, 1).astype(F32)
    after = shift(three.astype(BF16), -3).astype(F32)
    before = shift(pair.astype(BF16), 3).astype(F32)
    return three + after + before


def body(ham_blocks, neighbors, slice_widths, interval_index, start_vectors):
    rows_mine, columns = start_vectors.shape
    tiles = columns // TILE
    blocks, slots = ham_blocks.shape[:2]
    row_count = lax.axis_size("row")
    rows_all = blocks * BS * row_count
    panel_rows = blocks * BS
    span = panel_rows // 3
    turned = pl.pallas_call(
        turn_kernel,
        out_shape=shape((tiles, rows_mine, TILE)),
        in_specs=[pl.BlockSpec(memory_space=pltpu.HBM)],
        out_specs=pl.BlockSpec(memory_space=pltpu.HBM),
        scratch_shapes=[
            VMEM((tiles, rows_mine, TILE), BF16),
            pltpu.SemaphoreType.DMA((tiles,)),
            pltpu.SemaphoreType.DMA((tiles,)),
        ],
        compiler_params=pltpu.CompilerParams(vmem_limit_bytes=62 << 20),
    )(start_vectors)
    panel = lax.all_to_all(turned, "cuts", 0, 0).reshape(panel_rows, TILE)

    row = lax.axis_index("row")
    place = jnp.stack(
        [row * blocks, jnp.int32(blocks * row_count), lax.axis_index("cuts"), row % 2]
    ).astype(jnp.int32)
    near, far, pair = pl.pallas_call(
        table_kernel,
        out_shape=(
            shape((slots * blocks + 2,), jnp.int32),
            shape((2 * blocks // 3 * HB + 1,), jnp.int32),
            shape((tiles * REACH + LISTED,), jnp.int32),
        ),
        in_specs=smem(4),
        out_specs=tuple(smem(3)),
        compiler_params=pltpu.CompilerParams(vmem_limit_bytes=1 << 20),
        cost_estimate=pl.CostEstimate(flops=1 << 20, bytes_accessed=1 << 12, transcendentals=0),
    )(place, neighbors.T, slice_widths, interval_index)
    panel, near, far, pair = lax.optimization_barrier((panel, near, far, pair))
    work = 2 * blocks * slots * BS * BS * TILE
    outs = [shape((span, TILE)), shape((2, span, TILE), F32)]
    stacks = [VMEM((panel_rows, TILE), BF16), VMEM((panel_rows + BS, TILE), BF16)]

    def halos(inner, outer):
        from_outer = swap_outer(outer)
        return exchange(inner), from_outer

    def apply_first(field):
        inner, mid, outer = field
        from_inner, from_outer = halos(inner, outer)
        mid, edges, ham = pl.pallas_call(
            functools.partial(near_kernel, 1),
            out_shape=(*outs, shape(ham_blocks.shape)),
            in_specs=smem(1) + [pl.BlockSpec(memory_space=pltpu.HBM)] + vmem(3),
            out_specs=tuple(vmem(3)),
            scratch_shapes=[stacks[1], pltpu.SemaphoreType.DMA((FLIGHT,))],
            compiler_params=pltpu.CompilerParams(vmem_limit_bytes=40 << 20),
            cost_estimate=pl.CostEstimate(
                flops=work, bytes_accessed=ham_blocks.size * 2, transcendentals=0
            ),
        )(near, ham_blocks, inner, mid, outer)
        ham = pltpu.with_memory_space_constraint(ham, VMEM)
        return ham, (from_inner, from_outer, edges, mid)

    def apply_next(ham, field, before):
        inner, mid, outer = field
        from_inner, from_outer = halos(inner, outer)
        mid, edges = call(
            functools.partial(near_kernel, 2),
            outs,
            [near],
            [ham, inner, mid, outer, *before],
            stacks,
            work,
        )
        return from_inner, from_outer, edges, mid

    def edges_of(scale, ham, from_inner, from_outer, edges, mid):
        def side(outer, halo):
            (out,) = call(
                functools.partial(edge_kernel, scale, outer),
                [shape((span, TILE))],
                [far],
                [ham, halo, edges],
                [VMEM((span + BS, TILE), BF16)],
                work // 8,
            )
            return out

        outer = side(True, from_outer)
        return side(False, from_inner), mid, outer

    low, mid, high = (panel[q * span : (q + 1) * span] for q in range(3))
    even = row % 2 == 0
    start = (jnp.where(even, high, low), mid, jnp.where(even, low, high))
    ham, parts = apply_first(start)
    first = edges_of(1, ham, *parts)
    second = edges_of(2, ham, *apply_next(ham, first, start))
    from_inner, from_outer, edges, mid = apply_next(ham, second, first)
    (filtered,) = call(
        functools.partial(joined_kernel, 2),
        [shape((panel_rows, TILE))],
        [far],
        [ham, from_inner, from_outer, edges, mid],
        [VMEM((2, span + BS, TILE), BF16)],
        work // 4,
    )

    field = lax.all_to_all(filtered.reshape(tiles, rows_mine, TILE), "cuts", 0, 0)

    def gram(keep):
        return pl.pallas_call(
            functools.partial(gram_kernel, keep),
            out_shape=shape((HALF, TILE, TILE), F32 if keep else BF16),
            in_specs=[pl.BlockSpec(memory_space=pl.ANY)] + vmem(1),
            out_specs=pl.BlockSpec(memory_space=VMEM),
            scratch_shapes=[
                VMEM((tiles, TILE, rows_mine), BF16),
                SMEM(pair.shape, jnp.int32),
                pltpu.SemaphoreType.DMA((1,)),
            ],
            compiler_params=pltpu.CompilerParams(vmem_limit_bytes=24 << 20),
            cost_estimate=pl.CostEstimate(
                flops=1 << 28, bytes_accessed=1 << 21, transcendentals=0
            ),
        )(pair, field)

    partial = (gram(True) + exchange(gram(False)).astype(F32)).astype(BF16)
    cut_count = lax.axis_size("cuts")
    share = HALF * TILE // cut_count
    pieces = lax.all_to_all(partial.reshape(cut_count, share, TILE), "cuts", 0, 0)
    total = ring_total(jnp.sum(pieces.astype(F32), axis=0).astype(BF16))
    spread = jnp.broadcast_to(total.astype(BF16)[None], (cut_count, share, TILE))
    mine = lax.all_to_all(spread, "cuts", 0, 0).reshape(HALF, TILE, TILE)
    other = exchange(mine)
    (corrected,) = call(
        functools.partial(correct_kernel, rows_all),
        [shape((rows_mine, columns))],
        [pair],
        [field, mine, other],
        [
            VMEM((2 * HALF + 1, TILE, TILE), BF16),
            VMEM((tiles, TILE, TILE), BF16),
            VMEM((tiles, rows_mine, TILE), BF16),
            VMEM((tiles, TILE), F32),
        ],
        1 << 29,
    )
    return corrected


def solution(mesh):
    return jax.shard_map(
        body,
        mesh=mesh,
        in_specs=(P("row", None, None, None), P("row", None), P(), P(), P(("row", "cuts"), None)),
        out_specs=P(("row", "cuts"), None),
        check_vma=False,
    )
```

```python
import functools

import jax
import jax.numpy as jnp
from jax import lax
from jax.experimental import pallas as pl
from jax.experimental.pallas import tpu as pltpu
from jax.sharding import PartitionSpec as P

HB = 8
BS = 128
NINT = 8
TILE = 128
SIDE = 13
DIAG = 4
HALF = DIAG + 1 + SIDE
ZERO = 2 * HALF
LISTED = 63
FLIGHT = 4
REACH = 4
VMEM = pltpu.VMEM
SMEM = pltpu.SMEM
F32 = jnp.float32
BF16 = jnp.bfloat16


def vmem(count):
    return [pl.BlockSpec(memory_space=VMEM)] * count


def smem(count):
    return [pl.BlockSpec(memory_space=SMEM)] * count


def anywhere(count):
    return [pl.BlockSpec(memory_space=pl.ANY)] * count


def call(kernel, outs, scalars, arrays, scratch=(), flops=0, limit=24 << 20, fetch=False):
    moved = sum(a.size * a.dtype.itemsize for a in (*arrays, *outs))
    return pl.pallas_call(
        kernel,
        out_shape=tuple(outs),
        in_specs=(anywhere(1) if fetch else smem(len(scalars))) + vmem(len(arrays)),
        out_specs=tuple(vmem(len(outs))),
        scratch_shapes=list(scratch)
        + [SMEM(scalars[0].shape, jnp.int32), pltpu.SemaphoreType.DMA((1,))] * fetch,
        compiler_params=pltpu.CompilerParams(vmem_limit_bytes=limit),
        cost_estimate=pl.CostEstimate(flops=flops, bytes_accessed=moved, transcendentals=0),
    )(*scalars, *arrays)


def shape(dims, dtype=BF16):
    return jax.ShapeDtypeStruct(dims, dtype)


def table_kernel(where_ref, turned_ref, width_ref, interval_ref, near_ref, far_ref, pair_ref):
    slots, blocks = turned_ref.shape
    first, total, cut = where_ref[0], where_ref[1], where_ref[2]
    edge = blocks // 3

    def one_row(b, _):
        line = jnp.where(b < edge, b, b - edge)
        outer = (b < edge) | (b >= 2 * edge)

        @pl.when(outer)
        def _():
            for k in range(edge):
                far_ref[line * HB + k] = edge

        found = jnp.int32(0)
        for n in range(slots):
            away = turned_ref[n, b] - first
            away = jnp.where(away < -HB, away + total, away)
            away = jnp.where(away >= total - HB, away - total, away)
            local = (away >= 0) & (away < blocks)
            near_ref[n * blocks + b] = jnp.where(local, away, blocks)
            halo = jnp.where(away < 0, away + HB, away - blocks)

            @pl.when(jnp.logical_not(local))
            def _():
                far_ref[line * HB + found] = n * 16 + halo

            found += jnp.where(local, 0, 1)
        return 0

    lax.fori_loop(0, blocks, one_row, 0)
    tiles = (pair_ref.shape[0] - LISTED) // REACH
    listed = tiles * REACH + 1
    ends = []
    end = jnp.int32(0)
    for s in range(width_ref.shape[0]):
        end += width_ref[s] // TILE
        ends.append(end)

    def slice_of(t):
        index = jnp.int32(0)
        for end in ends:
            index += jnp.where(t >= end, 1, 0)
        return index

    lanes = [slice_of(t) for t in range(tiles)]
    found = jnp.int32(0)
    for m in range(2 * SIDE + 1):
        pair_ref[listed + m] = 1
    for i in range(tiles):
        for d in range(1, REACH):
            if i + d < tiles:
                valid = lanes[i + d] - lanes[i] <= 1
                slot = found + DIAG + 1 + jnp.where(found >= SIDE, DIAG + 1, 0)
                pair_ref[i * REACH + d] = jnp.where(valid, slot, ZERO)
                pair_ref[listed + jnp.where(valid, found, 2 * SIDE)] = i * REACH + d
                found += jnp.where(valid, 1, 0)
    core = where_ref[3]
    pair_ref[tiles * REACH] = core
    near_ref[slots * blocks] = core
    near_ref[slots * blocks + 1] = interval_ref[slice_of(cut)]
    far_ref[2 * edge * HB] = core


def turn_kernel(start_ref, out_ref, tiles_ref, read, written):
    tiles = out_ref.shape[0]

    def load(t):
        return pltpu.make_async_copy(
            start_ref.at[:, t * TILE : (t + 1) * TILE], tiles_ref.at[t], read.at[t]
        )

    def store(t):
        return pltpu.make_async_copy(tiles_ref.at[t], out_ref.at[t], written.at[t])

    for t in range(tiles):
        load(t).start()
    for t in range(tiles):
        load(t).wait()
        store(t).start()
    for t in range(tiles):
        store(t).wait()


def near_kernel(scale, near_ref, ham_ref, inner_ref, mid_ref, outer_ref, *rest):
    first = scale == 1
    blocks, slots = ham_ref.shape[:2]
    if first:
        mid_out, edge_out, ham_out, stack, loaded = rest
        chunk = blocks // loaded.shape[0]

        def load(c):
            rows = slice(c * chunk, (c + 1) * chunk)
            return pltpu.make_async_copy(ham_ref.at[rows], ham_out.at[rows], loaded.at[c])

        for c in range(FLIGHT):
            load(c).start()
        ham = ham_out
    else:
        mid_out, edge_out, before, stack = rest[-4:]
        ham = ham_ref
    third = blocks // 3
    span = third * BS
    core = near_ref[slots * blocks]
    inner_at, outer_at = (1 - core) * 2 * span, core * 2 * span

    def spread(inner, mid, outer, into):
        into[pl.ds(pl.multiple_of(inner_at, span), span)] = inner[...]
        into[pl.ds(pl.multiple_of(outer_at, span), span)] = outer[...]
        into[span : 2 * span] = mid[...]

    spread(inner_ref, mid_ref, outer_ref, stack)
    stack[blocks * BS :] = jnp.zeros((BS, TILE), BF16)
    if not first:
        spread(*rest[:3], before)
    centre = -0.5 + near_ref[slots * blocks + 1].astype(F32) * F32(1 / (NINT - 1))

    def tile_at(n, b):
        return stack[pl.ds(pl.multiple_of(near_ref[n * blocks + b] * BS, BS), BS), :]

    for b in range(blocks):
        if first and b % chunk == 0:
            c = b // chunk
            load(c).wait()
            if c + FLIGHT < blocks // chunk:
                load(c + FLIGHT).start()
        total = jnp.zeros((BS, TILE), F32)
        for n in range(0, slots, 2):
            if n + 1 < slots:
                left = jnp.concatenate([ham[b, n], ham[b, n + 1]], axis=1)
                right = jnp.concatenate([tile_at(n, b), tile_at(n + 1, b)], axis=0)
            else:
                left, right = ham[b, n], tile_at(n, b)
            total += jnp.dot(left, right, preferred_element_type=F32)
        part = b // third
        here = slice((b - part * third) * BS, (b - part * third + 1) * BS)
        own = stack[b * BS : (b + 1) * BS].astype(F32)
        value = total - centre * own
        if not first:
            value = scale * value - before[b * BS : (b + 1) * BS].astype(F32)
        if part == 1:
            mid_out[here, :] = value.astype(BF16)
        else:
            edge_out[part // 2, here, :] = value


def own_core():
    return lax.rem(lax.axis_index("row"), 2)


def lines_of(side, k, edge):
    return k + side * (edge - 1 - 2 * k), k + side * (3 * edge - 1 - 2 * k)


def add_outermost(scale, ham_ref, stack, edge_ref, total_ref, side, k, edge):
    index, b = lines_of(side, k, edge)
    here = pl.ds(pl.multiple_of(index * BS, BS), BS)
    part = jnp.dot(ham_ref[b, 2 - side], stack[here, :], preferred_element_type=F32)
    total_ref[k] = edge_ref[side, here, :] + scale * part


def add_listed(scale, far_ref, ham_ref, stack, total_ref, side, k, edge):
    index, b = lines_of(side, k, edge)
    left, right = [], []
    for slot_at in range(1, edge - k):
        entry = far_ref[(side * edge + index) * HB + slot_at]
        slot = entry // 16
        left.append(ham_ref[b, slot])
        start = pl.multiple_of((entry - slot * 16) * BS, BS)
        right.append(stack[pl.ds(start, BS), :])
    total = total_ref[k]
    for at in range(0, len(left), 2):
        lhs = jnp.concatenate(left[at : at + 2], axis=1)
        rhs = jnp.concatenate(right[at : at + 2], axis=0)
        total += scale * jnp.dot(lhs, rhs, preferred_element_type=F32)
    return index, total.astype(BF16)


def edge_kernel(scale, outer, table_ref, ham_ref, halo_ref, edge_ref, out_ref, stack, total_ref, far_ref, fetched):
    fetch = pltpu.make_async_copy(table_ref, far_ref, fetched.at[0])
    fetch.start()
    span = halo_ref.shape[0]
    edge = span // BS
    core = own_core()
    side = core if outer else 1 - core
    stack[:span] = halo_ref[...]
    stack[span:] = jnp.zeros((BS, TILE), BF16)
    for k in range(edge):
        add_outermost(scale, ham_ref, stack, edge_ref, total_ref, side, k, edge)
    fetch.wait()
    for k in range(edge):
        index, value = add_listed(scale, far_ref, ham_ref, stack, total_ref, side, k, edge)
        out_ref[pl.ds(pl.multiple_of(index * BS, BS), BS), :] = value


def joined_kernel(scale, table_ref, ham_ref, inner_ref, outer_ref, edge_ref, mid_ref, out_ref, stack, total_ref, far_ref, fetched):
    fetch = pltpu.make_async_copy(table_ref, far_ref, fetched.at[0])
    fetch.start()
    span = inner_ref.shape[0]
    edge = span // BS
    core = own_core()
    for side, ref in ((1 - core, inner_ref), (core, outer_ref)):
        stack[side, :span] = ref[...]
        stack[side, span:] = jnp.zeros((BS, TILE), BF16)
    out_ref[span : 2 * span, :] = mid_ref[...]
    for side in range(2):
        for k in range(edge):
            total = total_ref.at[side]
            add_outermost(scale, ham_ref, stack.at[side], edge_ref, total, side, k, edge)
    fetch.wait()
    for side in range(2):
        for k in range(edge):
            index, value = add_listed(
                scale, far_ref, ham_ref, stack.at[side], total_ref.at[side], side, k, edge
            )
            at = side * 2 * span + index * BS
            out_ref[at : at + BS, :] = value


def places():
    at_row = lax.broadcasted_iota(jnp.int32, (TILE, TILE), 0)
    at_col = lax.broadcasted_iota(jnp.int32, (TILE, TILE), 1)
    return at_row, at_col


def gram_kernel(keep, table_ref, field_ref, out_ref, turned, pair_ref, fetched):
    tiles = field_ref.shape[0]
    fetch = pltpu.make_async_copy(table_ref, pair_ref, fetched.at[0])
    fetch.start()
    at_row, at_col = places()
    for t in range(tiles):
        turned[t] = field_ref[t].T
    fetch.wait()
    core = pair_ref[tiles * REACH]
    half = core if keep else 1 - core

    def block(low, high):
        return jnp.dot(turned[low], field_ref[high], preferred_element_type=F32)

    extra = jnp.zeros((TILE, TILE), F32)
    for k in range(DIAG):
        tile = (half * DIAG + k) * 2
        upper = block(tile, tile)
        lower = block(tile + 1, tile + 1)
        squares = jnp.sum(jnp.where(at_row == at_col, lower, 0.0), axis=0, keepdims=True)
        extra = jnp.where(at_row == k, squares, extra)
        out_ref[k] = jnp.where(at_row <= at_col, upper, lower).astype(out_ref.dtype)
    out_ref[DIAG] = extra.astype(out_ref.dtype)
    for m in range(SIDE):
        code = pair_ref[tiles * REACH + 1 + half * SIDE + m]
        low = code // REACH
        high = low + code - low * REACH
        out_ref[DIAG + 1 + m] = block(low, high).astype(out_ref.dtype)


def correct_kernel(rows_all, table_ref, field_ref, mine_ref, other_ref, out_ref, gram, own, scaled, norm, pair_ref, fetched):
    fetch = pltpu.make_async_copy(table_ref, pair_ref, fetched.at[0])
    fetch.start()
    tiles = field_ref.shape[0]
    core = own_core()
    gram[pl.ds(core * HALF, HALF)] = mine_ref[...]
    gram[pl.ds(HALF - core * HALF, HALF)] = other_ref[...]
    gram[ZERO] = jnp.zeros((TILE, TILE), BF16)
    at_row, at_col = places()

    def prepare(t, block, squares):
        own[t] = block.astype(BF16)
        inverse = lax.rsqrt(squares / rows_all + 1e-05)
        norm[t : t + 1, :] = inverse
        scaled[t] = (field_ref[t].astype(F32) * (inverse * inverse)).astype(BF16)

    for q in range(tiles // 2):
        half, k = q // DIAG, q % DIAG
        packed = gram[half * HALF + k].astype(F32)
        flipped = packed.T
        upper = jnp.where(at_row <= at_col, packed, flipped)
        squares = jnp.sum(jnp.where(at_row == at_col, packed, 0.0), axis=0, keepdims=True)
        prepare(2 * q, upper, squares)
        squares = gram[half * HALF + DIAG].astype(F32)[k : k + 1, :]
        lower = jnp.where(at_row > at_col, packed, flipped)
        prepare(2 * q + 1, jnp.where(at_row == at_col, squares, lower), squares)
    fetch.wait()
    for j in range(tiles):
        below = range(max(0, j - REACH + 1), j)
        left = jnp.concatenate([scaled[i] for i in below] + [scaled[j]], axis=1)
        right = jnp.concatenate(
            [gram[pair_ref[i * REACH + j - i]] for i in below] + [own[j]], axis=0
        )
        total = jnp.dot(left, right, preferred_element_type=F32)
        above = range(j + 1, min(tiles, j + REACH))
        if above:
            left = jnp.concatenate([scaled[i] for i in above], axis=1)
            right = jnp.concatenate([gram[pair_ref[j * REACH + i - j]] for i in above], axis=1)
            total += lax.dot_general(
                left, right, (((1,), (1,)), ((), ())), preferred_element_type=F32
            )
        value = norm[j : j + 1, :] * (1.5 * field_ref[j].astype(F32) - (0.5 / rows_all) * total)
        out_ref[:, j * TILE : (j + 1) * TILE] = value.astype(BF16)


def shift(array, chips):
    size = lax.axis_size("row")
    return lax.ppermute(
        array, "row", [(i, (i + 2 * chips * (1 - 2 * (i % 2))) % size) for i in range(size)]
    )


def exchange(array):
    return lax.ppermute(array, "row", [(i, i ^ 1) for i in range(lax.axis_size("row"))])


def swap_outer(array):
    size = lax.axis_size("row")
    return lax.ppermute(array, "row", [(i, (i - 1 + 2 * (i % 2)) % size) for i in range(size)])


def ring_total(piece):
    own = piece.astype(F32)
    pair = own + shift(piece, -1).astype(F32)
    three = pair + shift(piece, 1).astype(F32)
    after = shift(three.astype(BF16), -3).astype(F32)
    before = shift(pair.astype(BF16), 3).astype(F32)
    return three + after + before


def body(ham_blocks, neighbors, slice_widths, interval_index, start_vectors):
    rows_mine, columns = start_vectors.shape
    tiles = columns // TILE
    blocks, slots = ham_blocks.shape[:2]
    row_count = lax.axis_size("row")
    rows_all = blocks * BS * row_count
    panel_rows = blocks * BS
    span = panel_rows // 3
    turned = pl.pallas_call(
        turn_kernel,
        out_shape=shape((tiles, rows_mine, TILE)),
        in_specs=[pl.BlockSpec(memory_space=pltpu.HBM)],
        out_specs=pl.BlockSpec(memory_space=pltpu.HBM),
        scratch_shapes=[
            VMEM((tiles, rows_mine, TILE), BF16),
            pltpu.SemaphoreType.DMA((tiles,)),
            pltpu.SemaphoreType.DMA((tiles,)),
        ],
        compiler_params=pltpu.CompilerParams(vmem_limit_bytes=62 << 20),
    )(start_vectors)
    panel = lax.all_to_all(turned, "cuts", 0, 0).reshape(panel_rows, TILE)

    row = lax.axis_index("row")
    place = jnp.stack(
        [row * blocks, jnp.int32(blocks * row_count), lax.axis_index("cuts"), row % 2]
    ).astype(jnp.int32)
    near, far, pair = pl.pallas_call(
        table_kernel,
        out_shape=(
            shape((slots * blocks + 2,), jnp.int32),
            shape((2 * blocks // 3 * HB + 128,), jnp.int32),
            shape((tiles * REACH + LISTED,), jnp.int32),
        ),
        in_specs=smem(4),
        out_specs=tuple(smem(3)),
        compiler_params=pltpu.CompilerParams(vmem_limit_bytes=1 << 20),
        cost_estimate=pl.CostEstimate(flops=1 << 20, bytes_accessed=1 << 12, transcendentals=0),
    )(place, neighbors.T, slice_widths, interval_index)
    panel, near, far, pair = lax.optimization_barrier((panel, near, far, pair))
    work = 2 * blocks * slots * BS * BS * TILE
    outs = [shape((span, TILE)), shape((2, span, TILE), F32)]
    stacks = [VMEM((panel_rows, TILE), BF16), VMEM((panel_rows + BS, TILE), BF16)]

    def halos(inner, outer):
        from_outer = swap_outer(outer)
        return exchange(inner), from_outer

    def apply_first(field):
        inner, mid, outer = field
        from_inner, from_outer = halos(inner, outer)
        mid, edges, ham = pl.pallas_call(
            functools.partial(near_kernel, 1),
            out_shape=(*outs, shape(ham_blocks.shape)),
            in_specs=smem(1) + [pl.BlockSpec(memory_space=pltpu.HBM)] + vmem(3),
            out_specs=tuple(vmem(3)),
            scratch_shapes=[stacks[1], pltpu.SemaphoreType.DMA((FLIGHT,))],
            compiler_params=pltpu.CompilerParams(vmem_limit_bytes=40 << 20),
            cost_estimate=pl.CostEstimate(
                flops=work, bytes_accessed=ham_blocks.size * 2, transcendentals=0
            ),
        )(near, ham_blocks, inner, mid, outer)
        ham = pltpu.with_memory_space_constraint(ham, VMEM)
        return ham, (from_inner, from_outer, edges, mid)

    def apply_next(ham, field, before):
        inner, mid, outer = field
        from_inner, from_outer = halos(inner, outer)
        mid, edges = call(
            functools.partial(near_kernel, 2),
            outs,
            [near],
            [ham, inner, mid, outer, *before],
            stacks,
            work,
        )
        return from_inner, from_outer, edges, mid

    def edges_of(scale, ham, from_inner, from_outer, edges, mid):
        def side(outer, halo):
            (out,) = call(
                functools.partial(edge_kernel, scale, outer),
                [shape((span, TILE))],
                [far],
                [ham, halo, edges],
                [VMEM((span + BS, TILE), BF16), VMEM((span // BS, BS, TILE), F32)],
                work // 8,
                fetch=True,
            )
            return out

        outer = side(True, from_outer)
        return side(False, from_inner), mid, outer

    low, mid, high = (panel[q * span : (q + 1) * span] for q in range(3))
    even = row % 2 == 0
    start = (jnp.where(even, high, low), mid, jnp.where(even, low, high))
    ham, parts = apply_first(start)
    first = edges_of(1, ham, *parts)
    second = edges_of(2, ham, *apply_next(ham, first, start))
    from_inner, from_outer, edges, mid = apply_next(ham, second, first)
    (filtered,) = call(
        functools.partial(joined_kernel, 2),
        [shape((panel_rows, TILE))],
        [far],
        [ham, from_inner, from_outer, edges, mid],
        [VMEM((2, span + BS, TILE), BF16), VMEM((2, span // BS, BS, TILE), F32)],
        work // 4,
        fetch=True,
    )

    field = lax.all_to_all(filtered.reshape(tiles, rows_mine, TILE), "cuts", 0, 0)

    def gram(keep):
        return pl.pallas_call(
            functools.partial(gram_kernel, keep),
            out_shape=shape((HALF, TILE, TILE), F32 if keep else BF16),
            in_specs=[pl.BlockSpec(memory_space=pl.ANY)] + vmem(1),
            out_specs=pl.BlockSpec(memory_space=VMEM),
            scratch_shapes=[
                VMEM((tiles, TILE, rows_mine), BF16),
                SMEM(pair.shape, jnp.int32),
                pltpu.SemaphoreType.DMA((1,)),
            ],
            compiler_params=pltpu.CompilerParams(vmem_limit_bytes=24 << 20),
            cost_estimate=pl.CostEstimate(
                flops=1 << 28, bytes_accessed=1 << 21, transcendentals=0
            ),
        )(pair, field)

    partial = (gram(True) + exchange(gram(False)).astype(F32)).astype(BF16)
    cut_count = lax.axis_size("cuts")
    share = HALF * TILE // cut_count
    pieces = lax.all_to_all(partial.reshape(cut_count, share, TILE), "cuts", 0, 0)
    total = ring_total(jnp.sum(pieces.astype(F32), axis=0).astype(BF16))
    spread = jnp.broadcast_to(total.astype(BF16)[None], (cut_count, share, TILE))
    mine = lax.all_to_all(spread, "cuts", 0, 0).reshape(HALF, TILE, TILE)
    other = exchange(mine)
    (corrected,) = call(
        functools.partial(correct_kernel, rows_all),
        [shape((rows_mine, columns))],
        [pair],
        [field, mine, other],
        [
            VMEM((2 * HALF + 1, TILE, TILE), BF16),
            VMEM((tiles, TILE, TILE), BF16),
            VMEM((tiles, rows_mine, TILE), BF16),
            VMEM((tiles, TILE), F32),
        ],
        1 << 29,
        fetch=True,
    )
    return corrected


def solution(mesh):
    return jax.shard_map(
        body,
        mesh=mesh,
        in_specs=(P("row", None, None, None), P("row", None), P(), P(), P(("row", "cuts"), None)),
        out_specs=P(("row", "cuts"), None),
        check_vma=False,
    )
```

```python
import functools

import jax
import jax.numpy as jnp
from jax import lax
from jax.experimental import pallas as pl
from jax.experimental.pallas import tpu as pltpu
from jax.sharding import PartitionSpec as P

HB = 8
BS = 128
NINT = 8
TILE = 128
SIDE = 13
DIAG = 4
HALF = DIAG + 1 + SIDE
ZERO = 2 * HALF
LISTED = 63
FLIGHT = 4
REACH = 4
VMEM = pltpu.VMEM
SMEM = pltpu.SMEM
F32 = jnp.float32
BF16 = jnp.bfloat16


def vmem(count):
    return [pl.BlockSpec(memory_space=VMEM)] * count


def smem(count):
    return [pl.BlockSpec(memory_space=SMEM)] * count


def anywhere(count):
    return [pl.BlockSpec(memory_space=pl.ANY)] * count


def call(kernel, outs, scalars, arrays, scratch=(), flops=0, limit=24 << 20, fetch=False):
    moved = sum(a.size * a.dtype.itemsize for a in (*arrays, *outs))
    return pl.pallas_call(
        kernel,
        out_shape=tuple(outs),
        in_specs=(anywhere(1) if fetch else smem(len(scalars))) + vmem(len(arrays)),
        out_specs=tuple(vmem(len(outs))),
        scratch_shapes=list(scratch)
        + [SMEM(scalars[0].shape, jnp.int32), pltpu.SemaphoreType.DMA((1,))] * fetch,
        compiler_params=pltpu.CompilerParams(vmem_limit_bytes=limit),
        cost_estimate=pl.CostEstimate(flops=flops, bytes_accessed=moved, transcendentals=0),
    )(*scalars, *arrays)


def shape(dims, dtype=BF16):
    return jax.ShapeDtypeStruct(dims, dtype)


def table_kernel(where_ref, turned_ref, width_ref, interval_ref, near_ref, far_ref, pair_ref):
    slots, blocks = turned_ref.shape
    first, total, cut = where_ref[0], where_ref[1], where_ref[2]
    edge = blocks // 3

    def one_row(b, _):
        line = jnp.where(b < edge, b, b - edge)
        outer = (b < edge) | (b >= 2 * edge)

        @pl.when(outer)
        def _():
            for k in range(edge):
                far_ref[line * HB + k] = edge

        found = jnp.int32(0)
        for n in range(slots):
            away = turned_ref[n, b] - first
            away = jnp.where(away < -HB, away + total, away)
            away = jnp.where(away >= total - HB, away - total, away)
            local = (away >= 0) & (away < blocks)
            near_ref[n * blocks + b] = jnp.where(local, away, blocks)
            halo = jnp.where(away < 0, away + HB, away - blocks)

            @pl.when(jnp.logical_not(local))
            def _():
                far_ref[line * HB + found] = n * 16 + halo

            found += jnp.where(local, 0, 1)
        return 0

    lax.fori_loop(0, blocks, one_row, 0)
    tiles = (pair_ref.shape[0] - LISTED) // REACH
    listed = tiles * REACH + 1
    ends = []
    end = jnp.int32(0)
    for s in range(width_ref.shape[0]):
        end += width_ref[s] // TILE
        ends.append(end)

    def slice_of(t):
        index = jnp.int32(0)
        for end in ends:
            index += jnp.where(t >= end, 1, 0)
        return index

    lanes = [slice_of(t) for t in range(tiles)]
    found = jnp.int32(0)
    for m in range(2 * SIDE + 1):
        pair_ref[listed + m] = 1
    for i in range(tiles):
        for d in range(1, REACH):
            if i + d < tiles:
                valid = lanes[i + d] - lanes[i] <= 1
                slot = found + DIAG + 1 + jnp.where(found >= SIDE, DIAG + 1, 0)
                pair_ref[i * REACH + d] = jnp.where(valid, slot, ZERO)
                pair_ref[listed + jnp.where(valid, found, 2 * SIDE)] = i * REACH + d
                found += jnp.where(valid, 1, 0)
    core = where_ref[3]
    pair_ref[tiles * REACH] = core
    near_ref[slots * blocks] = core
    near_ref[slots * blocks + 1] = interval_ref[slice_of(cut)]
    far_ref[2 * edge * HB] = core


def turn_kernel(start_ref, out_ref, tiles_ref, read, written):
    tiles = out_ref.shape[0]

    def load(t):
        return pltpu.make_async_copy(
            start_ref.at[:, t * TILE : (t + 1) * TILE], tiles_ref.at[t], read.at[t]
        )

    def store(t):
        return pltpu.make_async_copy(tiles_ref.at[t], out_ref.at[t], written.at[t])

    for t in range(tiles):
        load(t).start()
    for t in range(tiles):
        load(t).wait()
        store(t).start()
    for t in range(tiles):
        store(t).wait()


def near_kernel(scale, table_ref, ham_ref, inner_ref, mid_ref, outer_ref, *rest):
    *rest, near_ref, fetched = rest
    fetch = pltpu.make_async_copy(table_ref, near_ref, fetched.at[0])
    fetch.start()
    first = scale == 1
    blocks, slots = ham_ref.shape[:2]
    if first:
        mid_out, edge_out, ham_out, stack, loaded = rest
        chunk = blocks // loaded.shape[0]

        def load(c):
            rows = slice(c * chunk, (c + 1) * chunk)
            return pltpu.make_async_copy(ham_ref.at[rows], ham_out.at[rows], loaded.at[c])

        for c in range(FLIGHT):
            load(c).start()
        ham = ham_out
    else:
        mid_out, edge_out, before, stack = rest[-4:]
        ham = ham_ref
    third = blocks // 3
    span = third * BS
    core = own_core()
    inner_at, outer_at = (1 - core) * 2 * span, core * 2 * span

    def spread(inner, mid, outer, into):
        into[pl.ds(pl.multiple_of(inner_at, span), span)] = inner[...]
        into[pl.ds(pl.multiple_of(outer_at, span), span)] = outer[...]
        into[span : 2 * span] = mid[...]

    spread(inner_ref, mid_ref, outer_ref, stack)
    stack[blocks * BS :] = jnp.zeros((BS, TILE), BF16)
    if not first:
        spread(*rest[:3], before)
    fetch.wait()
    centre = -0.5 + near_ref[slots * blocks + 1].astype(F32) * F32(1 / (NINT - 1))

    def tile_at(n, b):
        return stack[pl.ds(pl.multiple_of(near_ref[n * blocks + b] * BS, BS), BS), :]

    for b in range(blocks):
        if first and b % chunk == 0:
            c = b // chunk
            load(c).wait()
            if c + FLIGHT < blocks // chunk:
                load(c + FLIGHT).start()
        total = jnp.zeros((BS, TILE), F32)
        for n in range(0, slots, 2):
            if n + 1 < slots:
                left = jnp.concatenate([ham[b, n], ham[b, n + 1]], axis=1)
                right = jnp.concatenate([tile_at(n, b), tile_at(n + 1, b)], axis=0)
            else:
                left, right = ham[b, n], tile_at(n, b)
            total += jnp.dot(left, right, preferred_element_type=F32)
        part = b // third
        here = slice((b - part * third) * BS, (b - part * third + 1) * BS)
        own = stack[b * BS : (b + 1) * BS].astype(F32)
        value = total - centre * own
        if not first:
            value = scale * value - before[b * BS : (b + 1) * BS].astype(F32)
        if part == 1:
            mid_out[here, :] = value.astype(BF16)
        else:
            edge_out[part // 2, here, :] = value


def own_core():
    return lax.rem(lax.axis_index("row"), 2)


def lines_of(side, k, edge):
    return k + side * (edge - 1 - 2 * k), k + side * (3 * edge - 1 - 2 * k)


def add_outermost(scale, ham_ref, stack, edge_ref, total_ref, side, k, edge):
    index, b = lines_of(side, k, edge)
    here = pl.ds(pl.multiple_of(index * BS, BS), BS)
    part = jnp.dot(ham_ref[b, 2 - side], stack[here, :], preferred_element_type=F32)
    total_ref[k] = edge_ref[side, here, :] + scale * part


def add_listed(scale, far_ref, ham_ref, stack, total_ref, side, k, edge):
    index, b = lines_of(side, k, edge)
    left, right = [], []
    for slot_at in range(1, edge - k):
        entry = far_ref[(side * edge + index) * HB + slot_at]
        slot = entry // 16
        left.append(ham_ref[b, slot])
        start = pl.multiple_of((entry - slot * 16) * BS, BS)
        right.append(stack[pl.ds(start, BS), :])
    total = total_ref[k]
    for at in range(0, len(left), 2):
        lhs = jnp.concatenate(left[at : at + 2], axis=1)
        rhs = jnp.concatenate(right[at : at + 2], axis=0)
        total += scale * jnp.dot(lhs, rhs, preferred_element_type=F32)
    return index, total.astype(BF16)


def edge_kernel(scale, outer, table_ref, ham_ref, halo_ref, edge_ref, out_ref, stack, total_ref, far_ref, fetched):
    fetch = pltpu.make_async_copy(table_ref, far_ref, fetched.at[0])
    fetch.start()
    span = halo_ref.shape[0]
    edge = span // BS
    core = own_core()
    side = core if outer else 1 - core
    stack[:span] = halo_ref[...]
    stack[span:] = jnp.zeros((BS, TILE), BF16)
    for k in range(edge):
        add_outermost(scale, ham_ref, stack, edge_ref, total_ref, side, k, edge)
    fetch.wait()
    for k in range(edge):
        index, value = add_listed(scale, far_ref, ham_ref, stack, total_ref, side, k, edge)
        out_ref[pl.ds(pl.multiple_of(index * BS, BS), BS), :] = value


def joined_kernel(scale, table_ref, ham_ref, inner_ref, outer_ref, edge_ref, mid_ref, out_ref, stack, total_ref, far_ref, fetched):
    fetch = pltpu.make_async_copy(table_ref, far_ref, fetched.at[0])
    fetch.start()
    span = inner_ref.shape[0]
    edge = span // BS
    core = own_core()
    for side, ref in ((1 - core, inner_ref), (core, outer_ref)):
        stack[side, :span] = ref[...]
        stack[side, span:] = jnp.zeros((BS, TILE), BF16)
    out_ref[span : 2 * span, :] = mid_ref[...]
    for side in range(2):
        for k in range(edge):
            total = total_ref.at[side]
            add_outermost(scale, ham_ref, stack.at[side], edge_ref, total, side, k, edge)
    fetch.wait()
    for side in range(2):
        for k in range(edge):
            index, value = add_listed(
                scale, far_ref, ham_ref, stack.at[side], total_ref.at[side], side, k, edge
            )
            at = side * 2 * span + index * BS
            out_ref[at : at + BS, :] = value


def places():
    at_row = lax.broadcasted_iota(jnp.int32, (TILE, TILE), 0)
    at_col = lax.broadcasted_iota(jnp.int32, (TILE, TILE), 1)
    return at_row, at_col


def gram_kernel(keep, table_ref, field_ref, out_ref, turned, pair_ref, fetched):
    tiles = field_ref.shape[0]
    fetch = pltpu.make_async_copy(table_ref, pair_ref, fetched.at[0])
    fetch.start()
    at_row, at_col = places()
    for t in range(tiles):
        turned[t] = field_ref[t].T
    fetch.wait()
    core = pair_ref[tiles * REACH]
    half = core if keep else 1 - core

    def block(low, high):
        return jnp.dot(turned[low], field_ref[high], preferred_element_type=F32)

    extra = jnp.zeros((TILE, TILE), F32)
    for k in range(DIAG):
        tile = (half * DIAG + k) * 2
        upper = block(tile, tile)
        lower = block(tile + 1, tile + 1)
        squares = jnp.sum(jnp.where(at_row == at_col, lower, 0.0), axis=0, keepdims=True)
        extra = jnp.where(at_row == k, squares, extra)
        out_ref[k] = jnp.where(at_row <= at_col, upper, lower).astype(out_ref.dtype)
    out_ref[DIAG] = extra.astype(out_ref.dtype)
    for m in range(SIDE):
        code = pair_ref[tiles * REACH + 1 + half * SIDE + m]
        low = code // REACH
        high = low + code - low * REACH
        out_ref[DIAG + 1 + m] = block(low, high).astype(out_ref.dtype)


def correct_kernel(rows_all, table_ref, field_ref, mine_ref, other_ref, out_ref, gram, own, scaled, norm, pair_ref, fetched):
    fetch = pltpu.make_async_copy(table_ref, pair_ref, fetched.at[0])
    fetch.start()
    tiles = field_ref.shape[0]
    core = own_core()
    gram[pl.ds(core * HALF, HALF)] = mine_ref[...]
    gram[pl.ds(HALF - core * HALF, HALF)] = other_ref[...]
    gram[ZERO] = jnp.zeros((TILE, TILE), BF16)
    at_row, at_col = places()

    def prepare(t, block, squares):
        own[t] = block.astype(BF16)
        inverse = lax.rsqrt(squares / rows_all + 1e-05)
        norm[t : t + 1, :] = inverse
        scaled[t] = (field_ref[t].astype(F32) * (inverse * inverse)).astype(BF16)

    for q in range(tiles // 2):
        half, k = q // DIAG, q % DIAG
        packed = gram[half * HALF + k].astype(F32)
        flipped = packed.T
        upper = jnp.where(at_row <= at_col, packed, flipped)
        squares = jnp.sum(jnp.where(at_row == at_col, packed, 0.0), axis=0, keepdims=True)
        prepare(2 * q, upper, squares)
        squares = gram[half * HALF + DIAG].astype(F32)[k : k + 1, :]
        lower = jnp.where(at_row > at_col, packed, flipped)
        prepare(2 * q + 1, jnp.where(at_row == at_col, squares, lower), squares)
    fetch.wait()
    for j in range(tiles):
        below = range(max(0, j - REACH + 1), j)
        left = jnp.concatenate([scaled[i] for i in below] + [scaled[j]], axis=1)
        right = jnp.concatenate(
            [gram[pair_ref[i * REACH + j - i]] for i in below] + [own[j]], axis=0
        )
        total = jnp.dot(left, right, preferred_element_type=F32)
        above = range(j + 1, min(tiles, j + REACH))
        if above:
            left = jnp.concatenate([scaled[i] for i in above], axis=1)
            right = jnp.concatenate([gram[pair_ref[j * REACH + i - j]] for i in above], axis=1)
            total += lax.dot_general(
                left, right, (((1,), (1,)), ((), ())), preferred_element_type=F32
            )
        value = norm[j : j + 1, :] * (1.5 * field_ref[j].astype(F32) - (0.5 / rows_all) * total)
        out_ref[:, j * TILE : (j + 1) * TILE] = value.astype(BF16)


def shift(array, chips):
    size = lax.axis_size("row")
    return lax.ppermute(
        array, "row", [(i, (i + 2 * chips * (1 - 2 * (i % 2))) % size) for i in range(size)]
    )


def exchange(array):
    return lax.ppermute(array, "row", [(i, i ^ 1) for i in range(lax.axis_size("row"))])


def swap_outer(array):
    size = lax.axis_size("row")
    return lax.ppermute(array, "row", [(i, (i - 1 + 2 * (i % 2)) % size) for i in range(size)])


def ring_total(piece):
    own = piece.astype(F32)
    pair = own + shift(piece, -1).astype(F32)
    three = pair + shift(piece, 1).astype(F32)
    after = shift(three.astype(BF16), -3).astype(F32)
    before = shift(pair.astype(BF16), 3).astype(F32)
    return three + after + before


def body(ham_blocks, neighbors, slice_widths, interval_index, start_vectors):
    rows_mine, columns = start_vectors.shape
    tiles = columns // TILE
    blocks, slots = ham_blocks.shape[:2]
    row_count = lax.axis_size("row")
    rows_all = blocks * BS * row_count
    panel_rows = blocks * BS
    span = panel_rows // 3
    turned = pl.pallas_call(
        turn_kernel,
        out_shape=shape((tiles, rows_mine, TILE)),
        in_specs=[pl.BlockSpec(memory_space=pltpu.HBM)],
        out_specs=pl.BlockSpec(memory_space=pltpu.HBM),
        scratch_shapes=[
            VMEM((tiles, rows_mine, TILE), BF16),
            pltpu.SemaphoreType.DMA((tiles,)),
            pltpu.SemaphoreType.DMA((tiles,)),
        ],
        compiler_params=pltpu.CompilerParams(vmem_limit_bytes=62 << 20),
    )(start_vectors)
    panel = lax.all_to_all(turned, "cuts", 0, 0).reshape(panel_rows, TILE)

    row = lax.axis_index("row")
    place = jnp.stack(
        [row * blocks, jnp.int32(blocks * row_count), lax.axis_index("cuts"), row % 2]
    ).astype(jnp.int32)
    near, far, pair = pl.pallas_call(
        table_kernel,
        out_shape=(
            shape((slots * blocks + 248,), jnp.int32),
            shape((2 * blocks // 3 * HB + 128,), jnp.int32),
            shape((tiles * REACH + LISTED,), jnp.int32),
        ),
        in_specs=smem(4),
        out_specs=tuple(smem(3)),
        compiler_params=pltpu.CompilerParams(vmem_limit_bytes=1 << 20),
        cost_estimate=pl.CostEstimate(flops=1 << 20, bytes_accessed=1 << 12, transcendentals=0),
    )(place, neighbors.T, slice_widths, interval_index)
    panel, near, far, pair = lax.optimization_barrier((panel, near, far, pair))
    work = 2 * blocks * slots * BS * BS * TILE
    outs = [shape((span, TILE)), shape((2, span, TILE), F32)]
    stacks = [VMEM((panel_rows, TILE), BF16), VMEM((panel_rows + BS, TILE), BF16)]

    def halos(inner, outer):
        from_outer = swap_outer(outer)
        return exchange(inner), from_outer

    def apply_first(field):
        inner, mid, outer = field
        from_inner, from_outer = halos(inner, outer)
        mid, edges, ham = pl.pallas_call(
            functools.partial(near_kernel, 1),
            out_shape=(*outs, shape(ham_blocks.shape)),
            in_specs=anywhere(1) + [pl.BlockSpec(memory_space=pltpu.HBM)] + vmem(3),
            out_specs=tuple(vmem(3)),
            scratch_shapes=[stacks[1], pltpu.SemaphoreType.DMA((FLIGHT,)), SMEM(near.shape, jnp.int32), pltpu.SemaphoreType.DMA((1,))],
            compiler_params=pltpu.CompilerParams(vmem_limit_bytes=40 << 20),
            cost_estimate=pl.CostEstimate(
                flops=work, bytes_accessed=ham_blocks.size * 2, transcendentals=0
            ),
        )(near, ham_blocks, inner, mid, outer)
        ham = pltpu.with_memory_space_constraint(ham, VMEM)
        return ham, (from_inner, from_outer, edges, mid)

    def apply_next(ham, field, before):
        inner, mid, outer = field
        from_inner, from_outer = halos(inner, outer)
        mid, edges = call(
            functools.partial(near_kernel, 2),
            outs,
            [near],
            [ham, inner, mid, outer, *before],
            stacks,
            work,
            fetch=True,
        )
        return from_inner, from_outer, edges, mid

    def edges_of(scale, ham, from_inner, from_outer, edges, mid):
        def side(outer, halo):
            (out,) = call(
                functools.partial(edge_kernel, scale, outer),
                [shape((span, TILE))],
                [far],
                [ham, halo, edges],
                [VMEM((span + BS, TILE), BF16), VMEM((span // BS, BS, TILE), F32)],
                work // 8,
                fetch=True,
            )
            return out

        outer = side(True, from_outer)
        return side(False, from_inner), mid, outer

    low, mid, high = (panel[q * span : (q + 1) * span] for q in range(3))
    even = row % 2 == 0
    start = (jnp.where(even, high, low), mid, jnp.where(even, low, high))
    ham, parts = apply_first(start)
    first = edges_of(1, ham, *parts)
    second = edges_of(2, ham, *apply_next(ham, first, start))
    from_inner, from_outer, edges, mid = apply_next(ham, second, first)
    (filtered,) = call(
        functools.partial(joined_kernel, 2),
        [shape((panel_rows, TILE))],
        [far],
        [ham, from_inner, from_outer, edges, mid],
        [VMEM((2, span + BS, TILE), BF16), VMEM((2, span // BS, BS, TILE), F32)],
        work // 4,
        fetch=True,
    )

    field = lax.all_to_all(filtered.reshape(tiles, rows_mine, TILE), "cuts", 0, 0)

    def gram(keep):
        return pl.pallas_call(
            functools.partial(gram_kernel, keep),
            out_shape=shape((HALF, TILE, TILE), F32 if keep else BF16),
            in_specs=[pl.BlockSpec(memory_space=pl.ANY)] + vmem(1),
            out_specs=pl.BlockSpec(memory_space=VMEM),
            scratch_shapes=[
                VMEM((tiles, TILE, rows_mine), BF16),
                SMEM(pair.shape, jnp.int32),
                pltpu.SemaphoreType.DMA((1,)),
            ],
            compiler_params=pltpu.CompilerParams(vmem_limit_bytes=24 << 20),
            cost_estimate=pl.CostEstimate(
                flops=1 << 28, bytes_accessed=1 << 21, transcendentals=0
            ),
        )(pair, field)

    partial = (gram(True) + exchange(gram(False)).astype(F32)).astype(BF16)
    cut_count = lax.axis_size("cuts")
    share = HALF * TILE // cut_count
    pieces = lax.all_to_all(partial.reshape(cut_count, share, TILE), "cuts", 0, 0)
    total = ring_total(jnp.sum(pieces.astype(F32), axis=0).astype(BF16))
    spread = jnp.broadcast_to(total.astype(BF16)[None], (cut_count, share, TILE))
    mine = lax.all_to_all(spread, "cuts", 0, 0).reshape(HALF, TILE, TILE)
    other = exchange(mine)
    (corrected,) = call(
        functools.partial(correct_kernel, rows_all),
        [shape((rows_mine, columns))],
        [pair],
        [field, mine, other],
        [
            VMEM((2 * HALF + 1, TILE, TILE), BF16),
            VMEM((tiles, TILE, TILE), BF16),
            VMEM((tiles, rows_mine, TILE), BF16),
            VMEM((tiles, TILE), F32),
        ],
        1 << 29,
        fetch=True,
    )
    return corrected


def solution(mesh):
    return jax.shard_map(
        body,
        mesh=mesh,
        in_specs=(P("row", None, None, None), P("row", None), P(), P(), P(("row", "cuts"), None)),
        out_specs=P(("row", "cuts"), None),
        check_vma=False,
    )
```
